32 devices in a mesh: pipe: 2 (over x), dp: 4 (over z), mp: 4 (over y, core).
Axes of the slice: x: 2, y: 2, z: 4, core: 2. Of those that a mesh axis runs over, the one named last changes fastest.
Arguments:
- section_in: bfloat16 [2, 12, 729, 1152], P('pipe', 'dp'), may hold values from -6 to 6
- ln1_gain: bfloat16 [2, 1152], P('pipe'), may hold values from 0.099609375 to 1.8984375
- ln1_bias: bfloat16 [2, 1152], P('pipe'), may hold values from -3 to 3
- qkv_weight: bfloat16 [2, 1152, 3, 1152], P('pipe', None, None, 'mp'), may hold values from -0.1875 to 0.1875
- qv_bias: bfloat16 [2, 2, 1152], P('pipe', None, 'mp'), may hold values from -3 to 3
- out_weight: bfloat16 [2, 1152, 1152], P('pipe', 'mp'), may hold values from -3 to 3
- out_bias: bfloat16 [2, 1152], P('pipe'), may hold values from -3 to 3
- ln2_gain: bfloat16 [2, 1152], P('pipe'), may hold values from 0.099609375 to 1.8984375
- ln2_bias: bfloat16 [2, 1152], P('pipe'), may hold values from -3 to 3
- fc1_weight: bfloat16 [2, 1152, 4304], P('pipe', None, 'mp'), may hold values from -0.1875 to 0.1875
- fc1_bias: bfloat16 [2, 4304], P('pipe', 'mp'), may hold values from -3 to 3
- fc2_weight: bfloat16 [2, 4304, 1152], P('pipe', 'mp'), may hold values from -0.1875 to 0.1875
- fc2_bias: bfloat16 [2, 1152], P('pipe'), may hold values from -4 to 4
Outputs:
- section_out: bfloat16 [2, 12, 729, 1152], P('pipe', 'dp')
- grad_ln1_gain: float32 [2, 1152], P('pipe')
- grad_ln1_bias: float32 [2, 1152], P('pipe')
- grad_qkv_weight: float32 [2, 1152, 3, 1152], P('pipe', None, None, 'mp')
- grad_qv_bias: float32 [2, 2, 1152], P('pipe', None, 'mp')
- grad_out_weight: float32 [2, 1152, 1152], P('pipe', 'mp')
- grad_out_bias: float32 [2, 1152], P('pipe')
- grad_ln2_gain: float32 [2, 1152], P('pipe')
- grad_ln2_bias: float32 [2, 1152], P('pipe')
- grad_fc1_weight: float32 [2, 1152, 4304], P('pipe', None, 'mp')
- grad_fc1_bias: float32 [2, 4304], P('pipe', 'mp')
- grad_fc2_weight: float32 [2, 4304, 1152], P('pipe', 'mp')
- grad_fc2_bias: float32 [2, 1152], P('pipe')
The draws below stay inside these ranges and needn't reach their ends.
All inputs are finite; a program needn't handle non-finite values.
Results may differ from the reference program's by a relative error of at most 0.028.
Values may be sent and summed in bfloat16 or wider, within the bound.
A program may use at most 320 MiB of HBM per device.

```python
import jax
import jax.numpy as jnp
from jax import lax

D = 1152
HEADS = 16
FF = 4304
SEQ = 729
HDIM = 72
IMAGES = 12
N_MP = 4


def steps_of(own_key, extent, shards, low, largest):
    loudness = 1.0
    for dim, blocks in shards:
        steps = jax.random.uniform(jax.random.fold_in(jax.random.fold_in(own_key, 6), dim), (blocks,), jnp.float32, low / len(shards), largest / len(shards))
        loudness = loudness * jnp.repeat(jnp.exp(steps), extent[dim] // blocks).reshape((-1,) + (1,) * (len(extent) - 1 - dim))
    return loudness


def noise(key, shape, spread, reach, pieces=(), kind=jnp.bfloat16):
    values = jax.random.normal(key, shape, jnp.float32) * spread
    if len(pieces) > 0:
        values = steps_of(key, shape, pieces, -0.22, 0.18) * values
    return jnp.clip(values, min=-reach, max=reach).astype(kind)


def setup_inputs(seed: int = 0) -> dict:
    arg_keys = jax.random.split(jax.random.key(seed), 14)
    section_in = noise(arg_keys[0], (2, IMAGES, SEQ, D), 1.0, 6.0, ((0, 2), (1, 4)))
    ln1_gain = jnp.clip(1.0 + 0.18 * jax.random.normal(arg_keys[1], (2, D), jnp.float32), 0.099609375, 1.8984375).astype(jnp.bfloat16)
    ln1_bias = noise(arg_keys[2], (2, D), 0.5, 3.0, ((0, 2),))
    qkv_weight = noise(arg_keys[3], (2, D, 3, D), D ** -0.5, 0.1875, ((0, 2), (3, 4)))
    qv_bias = noise(arg_keys[4], (2, 2, D), 0.5, 3.0, ((0, 2), (2, 4)))
    out_weight = noise(arg_keys[5], (2, D, D), (max(D // 256, 1)) ** -0.5, 3.0, ((0, 2), (1, 4)))
    out_bias = noise(arg_keys[6], (2, D), 0.5, 3.0, ((0, 2),))
    ln2_gain = jnp.clip(1.0 + 0.18 * jax.random.normal(arg_keys[7], (2, D), jnp.float32), 0.099609375, 1.8984375).astype(jnp.bfloat16)
    ln2_bias = noise(arg_keys[8], (2, D), 0.5, 3.0, ((0, 2),))
    fc1_weight = noise(arg_keys[9], (2, D, FF), D ** -0.5, 0.1875, ((0, 2), (2, 4)))
    fc1_bias = noise(arg_keys[10], (2, FF), 0.5, 3.0, ((0, 2), (1, 4)))
    fc2_weight = noise(arg_keys[11], (2, FF, D), (FF // 4) ** -0.5, 0.1875, ((0, 2), (1, 4)))
    fc2_bias = noise(arg_keys[12], (2, D), 1.0, 4.0, ((0, 2),))
    return dict(section_in=section_in, ln1_gain=ln1_gain, ln1_bias=ln1_bias, qkv_weight=qkv_weight, qv_bias=qv_bias, out_weight=out_weight, out_bias=out_bias, ln2_gain=ln2_gain, ln2_bias=ln2_bias, fc1_weight=fc1_weight, fc1_bias=fc1_bias, fc2_weight=fc2_weight, fc2_bias=fc2_bias)


@jax.custom_vjp
def low(v):
    return lax.optimization_barrier(v.astype(jnp.bfloat16)).astype(jnp.float32)

@jax.custom_vjp
def low_back(v):
    return v

def low_keep(v):
    return (low(v), None)

def low_pass(kept, grad):
    return (grad,)

def back_keep(v):
    return (v, None)

def back_low(kept, grad):
    return (low(grad),)
low.defvjp(low_keep, low_pass)
low_back.defvjp(back_keep, back_low)
PRECISE = lax.Precision.HIGHEST
EPSILON = 1e-06
GELU_SCALE = 0.7978845608028654
GELU_CUBIC = 0.044715

def norm_rows(values, gain_vec, shift_vec):
    center = values - lax.optimization_barrier(jnp.mean(values, axis=-1, keepdims=True))
    inv_std = lax.rsqrt(lax.optimization_barrier(jnp.mean(center * center, axis=-1, keepdims=True)) + EPSILON)
    return center * inv_std * gain_vec + shift_vec

def gelu_tanh(pre_act):
    return 0.5 * pre_act * (1.0 + jnp.tanh(GELU_SCALE * (pre_act + GELU_CUBIC * pre_act * pre_act * pre_act)))

def attend_image(triple):
    query, key_rows, value_rows = triple
    scores = jnp.einsum('qhd,khd->hqk', query, key_rows, precision=PRECISE) * HDIM ** (-0.5)
    scores = low_back(scores)
    row_max = lax.optimization_barrier(jnp.max(scores, axis=-1, keepdims=True))
    exp_terms = jnp.exp(scores - row_max)
    attn_probs = low(exp_terms / lax.optimization_barrier(jnp.sum(exp_terms, axis=-1, keepdims=True)))
    return jnp.einsum('hqk,khd->qhd', attn_probs, value_rows, precision=PRECISE)

def shard_sum(grouped, weight_groups):

    def add_group(running, pair):
        rows_part, weight_part = pair
        return (running + low(jnp.dot(rows_part, weight_part, precision=PRECISE)), None)
    start = jnp.zeros((grouped.shape[0], weight_groups.shape[2]), jnp.float32)
    return lax.scan(add_group, start, (jnp.swapaxes(grouped, 0, 1), weight_groups))[0]

def layer(stream, params):
    gain_one, shift_one, w_qkv, bias_qv, w_out, bias_out, gain_two, shift_two, w_fc1, bias_fc1, w_fc2, bias_fc2 = params
    row_count = stream.shape[0]
    normed = low(norm_rows(stream, gain_one, shift_one))
    packed = jnp.dot(normed, w_qkv.reshape(D, 3 * D), precision=PRECISE).reshape(row_count, 3, D)
    bias_three = jnp.stack([bias_qv[0], jnp.zeros_like(bias_qv[0]), bias_qv[1]])
    packed = low(low_back(packed + bias_three))
    shaped = packed.reshape(IMAGES, SEQ, 3, HEADS, HDIM)
    mixed = lax.map(jax.checkpoint(attend_image), (shaped[:, :, 0], shaped[:, :, 1], shaped[:, :, 2]))
    mixed = low(low_back(mixed.reshape(row_count, D)))
    branch = low_back(shard_sum(mixed.reshape(row_count, N_MP, D // N_MP), w_out.reshape(N_MP, D // N_MP, D)))
    mid_stream = stream + branch + bias_out
    normed_two = low(norm_rows(mid_stream, gain_two, shift_two))
    pre_act = low_back(jnp.dot(normed_two, w_fc1, precision=PRECISE) + bias_fc1)
    act_out = low(gelu_tanh(pre_act))
    branch_two = low_back(shard_sum(act_out.reshape(row_count, N_MP, FF // N_MP), w_fc2.reshape(N_MP, FF // N_MP, D)))
    return mid_stream + branch_two + bias_fc2

def reference(section_in, ln1_gain, ln1_bias, qkv_weight, qv_bias, out_weight, out_bias, ln2_gain, ln2_bias, fc1_weight, fc1_bias, fc2_weight, fc2_bias):
    params = tuple((item.astype(jnp.float32) for item in (ln1_gain, ln1_bias, qkv_weight, qv_bias, out_weight, out_bias, ln2_gain, ln2_bias, fc1_weight, fc1_bias, fc2_weight, fc2_bias)))
    row_count = IMAGES * SEQ
    source = section_in[0].astype(jnp.float32).reshape(row_count, D)
    cotangent = section_in[1].astype(jnp.float32).reshape(row_count, D)

    def forward(source_rows, weights):
        stream = low_back(source_rows)
        stream = layer(stream, tuple((item[0] for item in weights)))
        stream = low(low_back(stream))
        return layer(stream, tuple((item[1] for item in weights)))
    result, pullback = jax.vjp(forward, source, params)
    grad_source, grad_params = pullback(cotangent)
    section_out = jnp.stack([grad_source.astype(jnp.bfloat16), result.astype(jnp.bfloat16)]).reshape(2, IMAGES, SEQ, D)
    return (section_out, grad_params[0], grad_params[1], grad_params[2], grad_params[3], grad_params[4], grad_params[5], grad_params[6], grad_params[7], grad_params[8], grad_params[9], grad_params[10], grad_params[11])
```

```python
import functools

import jax
import jax.numpy as jnp
from jax import lax
from jax.experimental import pallas as pl
from jax.experimental.pallas import tpu as pltpu
from jax.sharding import PartitionSpec as P

HDIM = 72
HPAD = 128
EPSILON = 1e-06
GELU_SCALE = 0.7978845608028654
GELU_CUBIC = 0.044715
MESH = pl.DeviceIdType.MESH
BF = jnp.bfloat16
F32 = jnp.float32
CHUNK = 256
HALF = CHUNK // 2
VMEM_LIMIT = 67043328


def dot_nn(a, b):
    return lax.dot_general(a, b, (((1,), (0,)), ((), ())), preferred_element_type=F32)


def dot_nt(a, b):
    return lax.dot_general(a, b, (((1,), (1,)), ((), ())), preferred_element_type=F32)


def dot_tn(a, b):
    return lax.dot_general(a, b, (((0,), (0,)), ((), ())), preferred_element_type=F32)


def col_sum(v):
    return jnp.sum(v, axis=0, keepdims=True)


def norm_stats(v):
    center = v - jnp.mean(v, axis=-1, keepdims=True)
    inv = lax.rsqrt(jnp.mean(center * center, axis=-1, keepdims=True) + EPSILON)
    return center * inv, inv


def norm_back(e, hat, inv, gain):
    d_hat = e * gain
    mean_d = jnp.mean(d_hat, axis=-1, keepdims=True)
    mean_dx = jnp.mean(d_hat * hat, axis=-1, keepdims=True)
    return inv * (d_hat - mean_d - hat * mean_dx)


class Spot:
    def __init__(self, rows):
        self.stage = lax.axis_index("pipe")
        me = lax.axis_index("mp")
        self.rows = rows
        self.core = lax.rem(me, 2)
        self.row = lax.div(me, 2)
        self.sib = self.row * 2 + (1 - self.core)
        self.piece = HALF // rows

    def ahead(self, j):
        return lax.rem(self.row + j, self.rows)

    def behind(self, j):
        return lax.rem(self.row + self.rows - j, self.rows)

    def peer(self, row):
        return {"mp": row * 2 + self.core}


def enter(spot):
    barrier = pltpu.get_barrier_semaphore()
    targets = [{"mp": spot.sib}, {"pipe": 1 - spot.stage}]
    targets += [spot.peer(spot.ahead(j)) for j in range(1, spot.rows)]
    for target in targets:
        pl.semaphore_signal(barrier, inc=1, device_id=target, device_id_type=MESH)
    pl.semaphore_wait(barrier, len(targets))


def remote(src, dst, send, recv, target):
    return pltpu.make_async_remote_copy(
        src_ref=src, dst_ref=dst, send_sem=send, recv_sem=recv, device_id=target, device_id_type=MESH
    )


class Gather:
    def __init__(self, buf, ssem, rsem, kind, spot):
        self.buf, self.ssem, self.rsem, self.kind, self.spot = buf, ssem, rsem, kind, spot

    def view(self, c, row):
        p = self.spot.piece
        start = c * CHUNK + self.spot.core * HALF + row * p
        return self.buf.at[pl.ds(pl.multiple_of(start, p), p)]

    def mine(self, c):
        return self.view(c, self.spot.row)

    def copy(self, c, which, view, target):
        k = self.kind + which
        return remote(view, view, self.ssem.at[k, c], self.rsem.at[k, c], target)

    def near_copy(self, c):
        return self.copy(c, 0, self.mine(c), {"mp": self.spot.sib})

    def far_copy(self, c, j):
        return self.copy(c, 2 * j - 1, self.mine(c), self.spot.peer(self.spot.ahead(j)))

    def pass_copy(self, c, j):
        return self.copy(c, 2 * j, self.view(c, self.spot.behind(j)), {"mp": self.spot.sib})

    def start(self, c):
        for j in range(1, self.spot.rows):
            self.far_copy(c, j).start()
        self.near_copy(c).start()

    def forward(self, c):
        for j in range(1, self.spot.rows):
            self.far_copy(c, j).wait_recv()
            self.pass_copy(c, j).start()

    def finish(self, c):
        self.near_copy(c).wait_recv()
        for j in range(1, self.spot.rows):
            self.pass_copy(c, j).wait_recv()

    def drain(self, c):
        self.near_copy(c).wait_send()
        for j in range(1, self.spot.rows):
            self.far_copy(c, j).wait_send()
            self.pass_copy(c, j).wait_send()


class Reduce:
    def __init__(self, part, near, out, far, ssem, rsem, kind, spot):
        self.part, self.near, self.out, self.far = part, near, out, far
        self.ssem, self.rsem, self.kind, self.spot = ssem, rsem, kind, spot

    def near_copy(self, c):
        src = self.part.at[c, pl.ds(pl.multiple_of((1 - self.spot.core) * HALF, HALF), HALF)]
        k = self.kind
        return remote(src, self.near.at[c], self.ssem.at[k, c], self.rsem.at[k, c], {"mp": self.spot.sib})

    def far_copy(self, c, j):
        k = self.kind + j
        target = self.spot.peer(self.spot.ahead(j))
        return remote(
            self.out.at[c, j - 1], self.far.at[c, j - 1], self.ssem.at[k, c], self.rsem.at[k, c], target
        )

    def start(self, c, value):
        self.part[c] = value.astype(BF)
        self.near_copy(c).start()

    def pair(self, c, row):
        p = self.spot.piece
        own = self.part[c, pl.ds(pl.multiple_of(self.spot.core * HALF + row * p, p), p)]
        near = self.near[c, pl.ds(pl.multiple_of(row * p, p), p)]
        return own.astype(F32) + near.astype(F32)

    def cross(self, c):
        self.near_copy(c).wait_recv()
        for j in range(1, self.spot.rows):
            self.out[c, j - 1] = self.pair(c, self.spot.ahead(j)).astype(BF)
            self.far_copy(c, j).start()

    def result(self, c):
        total = self.pair(c, self.spot.row)
        for j in range(1, self.spot.rows):
            self.far_copy(c, j).wait_recv()
            total = total + self.far[c, j - 1].astype(F32)
        return total

    def drain(self, c):
        self.near_copy(c).wait_send()
        for j in range(1, self.spot.rows):
            self.far_copy(c, j).wait_send()


def forward_kernel(
    images, chunks, heads, length, scaling, rows_mp,
    x_hbm, vec, bqkv, wqkv, wout, w1, w2,
    y_o, xin_o, a1_o, qkv_o, o_o, lse_o, a2_o, g_o, sl_o, h1_o,
    xbuf, a1b, qkvb, ob, lseb, a2b, gb, slb, h1b, outb,
    part1, near1, out1, far1, part2, near2, out2, far2,
    ssem, rsem, psend, precv, lsem,
):
    spot = Spot(rows_mp)
    stage, piece = spot.stage, spot.piece
    hw = heads * HPAD

    load = pltpu.make_async_copy(x_hbm, xbuf, lsem.at[0])

    @pl.when(stage == 0)
    def _():
        load.start()

    enter(spot)
    kinds = sem_kinds(rows_mp)
    gat2 = Gather(a2b, ssem, rsem, kinds[1], spot)
    red1 = Reduce(part1, near1, out1, far1, ssem, rsem, kinds[2], spot)
    red2 = Reduce(part2, near2, out2, far2, ssem, rsem, kinds[3], spot)

    def gat1(i):
        return Gather(a1b.at[lax.rem(i, 2)], ssem, rsem, kinds[0], spot)

    def vrow(r):
        return vec[r : r + 1, :]

    def pipe_copy(i, c):
        return remote(
            outb.at[pl.ds(c * piece, piece)],
            xbuf.at[i, pl.ds(c * piece, piece)],
            psend.at[c],
            precv.at[i, c],
            {"pipe": 1},
        )

    def y_copy(i, c):
        return pltpu.make_async_copy(
            outb.at[pl.ds(c * piece, piece)], y_o.at[i, pl.ds(c * piece, piece)], psend.at[c]
        )

    def begin(i, c):
        @pl.when(stage == 1)
        def _():
            pipe_copy(i, c).wait_recv()

        v = xbuf[i, pl.ds(c * piece, piece)].astype(F32)
        hat, _ = norm_stats(v)
        gat1(i).mine(c)[...] = (hat * vrow(0) + vrow(1)).astype(BF)
        gat1(i).start(c)

    def project(i, c):
        gat1(i).finish(c)
        a = a1b[lax.rem(i, 2), pl.ds(c * CHUNK, CHUNK)]
        qkvb[pl.ds(c * CHUNK, CHUNK)] = (dot_nt(a, wqkv[...]) + bqkv[...]).astype(BF)

    def attend(c):
        rows = pl.ds(c * CHUNK, CHUNK)
        total = chunks * CHUNK
        valid = lax.broadcasted_iota(jnp.int32, (CHUNK, total), 1) < length
        lane = lax.broadcasted_iota(jnp.int32, (CHUNK, HPAD), 1)
        kept = jnp.zeros((CHUNK, HPAD), F32)
        for h in range(heads):
            q = qkvb[rows, h * HPAD : (h + 1) * HPAD]
            k = qkvb[:, hw + h * HPAD : hw + (h + 1) * HPAD]
            v = qkvb[:, 2 * hw + h * HPAD : 2 * hw + (h + 1) * HPAD]
            s = jnp.where(valid, dot_nt(q, k) * scaling, -1e30)
            m = jnp.max(s, axis=-1, keepdims=True)
            e = jnp.exp(s - m)
            t = jnp.sum(e, axis=-1, keepdims=True)
            p = (e / t).astype(BF)
            ob[rows, h * HPAD : (h + 1) * HPAD] = dot_nn(p, v).astype(BF)
            kept = jnp.where(lane == h, m + jnp.log(t), kept)
        lseb[rows] = kept
        red1.start(c, dot_nn(ob[rows], wout[...]))

    def middle(i, c):
        sl = pl.ds(c * piece, piece)
        h1 = xbuf[i, sl].astype(F32) + red1.result(c) + vrow(2)
        h1b[sl] = h1
        hat, _ = norm_stats(h1)
        gat2.mine(c)[...] = (hat * vrow(3) + vrow(4)).astype(BF)
        gat2.start(c)

    def feed(c):
        rows = pl.ds(c * CHUNK, CHUNK)
        gat2.finish(c)
        u = dot_nt(a2b[rows], w1[...]) + vec[5:6, 0 : w1.shape[0]]
        uu = u * u
        t = jnp.tanh(GELU_SCALE * (u + GELU_CUBIC * uu * u))
        half = 0.5 * (1.0 + t)
        gb[rows] = (u * half).astype(BF)
        slb[rows] = (
            half + 0.5 * u * (1.0 - t * t) * (GELU_SCALE * (1.0 + 3.0 * GELU_CUBIC * uu))
        ).astype(BF)
        red2.start(c, dot_nn(gb[rows], w2[...]))

    def end(i, c):
        sl = pl.ds(c * piece, piece)
        outb[sl] = (h1b[sl] + red2.result(c) + vrow(6)).astype(BF)

        @pl.when(stage == 0)
        def _():
            pipe_copy(i, c).start()

        @pl.when(stage == 1)
        def _():
            y_copy(i, c).start()

    def end_wait(i, c):
        @pl.when(stage == 0)
        def _():
            pipe_copy(i, c).wait_send()

        @pl.when(stage == 1)
        def _():
            y_copy(i, c).wait()

    def saves(i):
        return [
            pltpu.make_async_copy(a, b, lsem.at[1 + n])
            for n, (a, b) in enumerate(
                (
                    (a1b.at[lax.rem(i, 2)], a1_o.at[i]),
                    (qkvb, qkv_o.at[i]),
                    (ob, o_o.at[i]),
                    (lseb, lse_o.at[i]),
                    (a2b, a2_o.at[i]),
                    (gb, g_o.at[i]),
                    (slb, sl_o.at[i]),
                    (h1b, h1_o.at[i]),
                    (xbuf.at[i], xin_o.at[i]),
                )
            )
        ]

    @pl.when(stage == 0)
    def _():
        load.wait()

    every = range(chunks)

    def first(i):
        for c in every:
            begin(i, c)

    def second(i):
        for c in every:
            gat1(i).forward(c)
        for c in every:
            project(i, c)
        for c in every:
            gat1(i).drain(c)

    first(0)
    second(0)

    def image(i, carry):
        sv = saves(i)
        sv[0].start()
        sv[1].start()
        for s in range(chunks + 6):
            def at(j):
                return s - j if 0 <= s - j < chunks else None

            c = at(0)
            if c is not None:
                attend(c)
            c = at(1)
            if c is not None:
                red1.cross(c)
            c = at(5)
            if c is not None:
                red2.cross(c)
            c = at(2)
            if c is not None:
                middle(i, c)
            c = at(3)
            if c is not None:
                gat2.forward(c)
            c = at(6)
            if c is not None:
                end(i, c)
            c = at(4)
            if c is not None:
                feed(c)
            if s == chunks:
                sv[2].start()
                sv[3].start()
        for n in range(4, 9):
            sv[n].start()
        for n in range(9):
            sv[n].wait()

        @pl.when(i + 1 < images)
        def _():
            first(i + 1)

        for c in every:
            red1.drain(c)
            red2.drain(c)
            gat2.drain(c)
            end_wait(i, c)

        @pl.when(i + 1 < images)
        def _():
            second(i + 1)

        return carry

    lax.fori_loop(0, images, image, 0)


def backward_kernel(
    images, chunks, heads, length, scaling, rows_mp,
    d_hbm, vec, wqkv, wout, w1, w2,
    xin_i, a1_i, qkv_i, o_i, lse_i, a2_i, g_i, sl_i, h1_i,
    dx_o, gqkv, gout, g1, g2, small, gbqkv,
    dbuf, xinb, a1b, qkvb, ob, lseb, a2b, gb, slb, h1b, dmb, dab, dqb, dkv, dob, outb,
    part1, near1, out1, far1, part2, near2, out2, far2,
    ssem, rsem, psend, precv, lsem,
):
    spot = Spot(rows_mp)
    stage, piece = spot.stage, spot.piece
    hw = heads * HPAD
    load = pltpu.make_async_copy(d_hbm, dbuf, lsem.at[0])

    @pl.when(stage == 1)
    def _():
        load.start()

    def loads(i):
        return [
            pltpu.make_async_copy(b, a, lsem.at[1 + n])
            for n, (a, b) in enumerate(
                (
                    (a1b, a1_i.at[i]),
                    (qkvb, qkv_i.at[i]),
                    (ob, o_i.at[i]),
                    (lseb, lse_i.at[i]),
                    (a2b, a2_i.at[i]),
                    (gb, g_i.at[i]),
                    (slb, sl_i.at[i]),
                    (h1b, h1_i.at[i]),
                    (xinb, xin_i.at[i]),
                )
            )
        ]

    for ld in loads(0):
        ld.start()
    enter(spot)
    kinds = sem_kinds(rows_mp)
    gatm = Gather(dmb, ssem, rsem, kinds[0], spot)
    gata = Gather(dab, ssem, rsem, kinds[1], spot)
    red1 = Reduce(part1, near1, out1, far1, ssem, rsem, kinds[2], spot)
    red2 = Reduce(part2, near2, out2, far2, ssem, rsem, kinds[3], spot)
    every = range(chunks)

    gqkv[...] = jnp.zeros_like(gqkv)
    gout[...] = jnp.zeros_like(gout)
    g1[...] = jnp.zeros_like(g1)
    g2[...] = jnp.zeros_like(g2)
    small[...] = jnp.zeros_like(small)
    gbqkv[...] = jnp.zeros_like(gbqkv)

    def add(r, v):
        small[r : r + 1, :] += v

    def pipe_copy(i, c):
        return remote(
            outb.at[pl.ds(c * piece, piece)],
            dbuf.at[i, pl.ds(c * piece, piece)],
            psend.at[c],
            precv.at[i, c],
            {"pipe": 0},
        )

    def x_copy(i, c):
        return pltpu.make_async_copy(
            outb.at[pl.ds(c * piece, piece)], dx_o.at[i, pl.ds(c * piece, piece)], psend.at[c]
        )

    def begin(i, c):
        @pl.when(stage == 0)
        def _():
            pipe_copy(i, c).wait_recv()

        v = dbuf[i, pl.ds(c * piece, piece)]
        gatm.mine(c)[...] = v
        gatm.start(c)
        add(6, col_sum(v.astype(F32)))

    def feed(c):
        rows = pl.ds(c * CHUNK, CHUNK)
        gatm.finish(c)
        du = (dot_nt(dmb[rows], w2[...]) * slb[rows].astype(F32)).astype(BF)
        slb[rows] = du
        small[5:6, 0 : w1.shape[0]] += col_sum(du.astype(F32))
        red1.start(c, dot_nn(du, w1[...]))

    def middle(i, c):
        sl = pl.ds(c * piece, piece)
        e = red1.result(c)
        hat, inv = norm_stats(h1b[sl])
        add(3, col_sum(e * hat))
        add(4, col_sum(e))
        dh = dbuf[i, sl].astype(F32) + norm_back(e, hat, inv, vec[3:4, :])
        h1b[sl] = dh
        add(2, col_sum(dh))
        gata.mine(c)[...] = dh.astype(BF)
        gata.start(c)

    def weights(acc, a, b, step):
        def tile(n, carry):
            cols = pl.ds(pl.multiple_of(n * step, step), step)
            acc[cols] += dot_tn(a[:, cols], b[...])
            return carry

        lax.fori_loop(0, acc.shape[0] // step, tile, 0)

    def attend(c):
        rows = pl.ds(c * CHUNK, CHUNK)
        total = chunks * CHUNK
        valid = lax.broadcasted_iota(jnp.int32, (CHUNK, total), 1) < length
        gata.finish(c)
        dob[...] = dot_nt(dab[rows], wout[...]).astype(BF)
        for h in range(heads):
            cq = slice(h * HPAD, (h + 1) * HPAD)
            ck = slice(hw + h * HPAD, hw + (h + 1) * HPAD)
            cv = slice(2 * hw + h * HPAD, 2 * hw + (h + 1) * HPAD)
            q, k, v = qkvb[rows, cq], qkvb[:, ck], qkvb[:, cv]
            d = dob[:, cq]
            s = dot_nt(q, k) * scaling
            p = jnp.where(valid, jnp.exp(s - lseb[rows, h : h + 1]), 0.0)
            dv = dot_tn(p.astype(BF), d)
            dp = dot_nt(d, v)
            inner = jnp.sum(dp * p, axis=-1, keepdims=True)
            ds = (p * (dp - inner)).astype(BF)
            dq = (dot_nn(ds, k) * scaling).astype(BF)
            dqb[rows, cq] = dq
            gbqkv[0:1, cq] += col_sum(dq.astype(F32))
            dk = dot_tn(ds, q)
            if c == 0:
                dkv[:, cq] = dk
                dkv[:, ck] = dv
            else:
                dkv[:, cq] += dk
                dkv[:, ck] += dv

    def close():
        dk = (dkv[:, 0:hw] * scaling).astype(BF)
        dqb[:, hw : 2 * hw] = dk
        dv = dkv[:, hw : 2 * hw].astype(BF)
        dqb[:, 2 * hw : 3 * hw] = dv
        gbqkv[0:1, 2 * hw : 3 * hw] += col_sum(dv.astype(F32))

    def unproject(c):
        rows = pl.ds(c * CHUNK, CHUNK)
        red2.start(c, dot_nn(dqb[rows], wqkv[...]))

    def end(i, c):
        sl = pl.ds(c * piece, piece)
        e = red2.result(c)
        hat, inv = norm_stats(xinb[sl].astype(F32))
        add(0, col_sum(e * hat))
        add(1, col_sum(e))
        outb[sl] = (h1b[sl] + norm_back(e, hat, inv, vec[0:1, :])).astype(BF)

        @pl.when(stage == 1)
        def _():
            pipe_copy(i, c).start()

        @pl.when(stage == 0)
        def _():
            x_copy(i, c).start()

    def end_wait(i, c):
        @pl.when(stage == 1)
        def _():
            pipe_copy(i, c).wait_send()

        @pl.when(stage == 0)
        def _():
            x_copy(i, c).wait()

    @pl.when(stage == 1)
    def _():
        load.wait()

    def image(i, carry):
        ld = loads(i)
        for c in every:
            begin(i, c)
        for c in every:
            gatm.forward(c)
        for n in (5, 6):
            ld[n].wait()
        for c in every:
            feed(c)
            if c >= 1:
                red1.cross(c - 1)
        for n in (0, 1, 2, 3, 4, 7, 8):
            ld[n].wait()
        middle(i, 0)
        red1.cross(chunks - 1)
        for c in range(1, chunks - 1):
            middle(i, c)
        for c in every:
            gatm.drain(c)
        weights(g2, gb, dmb, HPAD)
        middle(i, chunks - 1)
        for c in every:
            gata.forward(c)
        weights(g1, slb, a2b, HPAD)
        for c in every:
            attend(c)
        close()
        for c in every:
            unproject(c)
            if c >= 1:
                red2.cross(c - 1)
        red2.cross(chunks - 1)
        for c in range(chunks - 1):
            end(i, c)
        weights(gout, ob, dab, HPAD)
        end(i, chunks - 1)
        weights(gqkv, dqb, a1b, HPAD)
        for c in every:
            gata.drain(c)
            red1.drain(c)
            red2.drain(c)
            end_wait(i, c)

        @pl.when(i + 1 < images)
        def _():
            for nx in loads(i + 1):
                nx.start()

        return carry

    lax.fori_loop(0, images, image, 0)


def vmem():
    return pl.BlockSpec(memory_space=pltpu.VMEM)


def anywhere():
    return pl.BlockSpec(memory_space=pl.ANY)


def comm_scratch(chunks, width, rows_mp):
    one = [
        pltpu.VMEM((chunks, CHUNK, width), BF),
        pltpu.VMEM((chunks, HALF, width), BF),
        pltpu.VMEM((chunks, rows_mp - 1, HALF // rows_mp, width), BF),
        pltpu.VMEM((chunks, rows_mp - 1, HALF // rows_mp, width), BF),
    ]
    return one + one


def sem_kinds(rows_mp):
    gather = 2 * rows_mp - 1
    return 0, gather, 2 * gather, 2 * gather + rows_mp


def sems(images, chunks, rows_mp):
    dma = pltpu.SemaphoreType.DMA
    kinds = 6 * rows_mp - 2
    return [dma((kinds, chunks)), dma((kinds, chunks)), dma((chunks,)), dma((images, chunks)), dma((10,))]


def on_device(
    section_in,
    ln1_gain,
    ln1_bias,
    qkv_weight,
    qv_bias,
    out_weight,
    out_bias,
    ln2_gain,
    ln2_bias,
    fc1_weight,
    fc1_bias,
    fc2_weight,
    fc2_bias,
):
    stage = lax.axis_index("pipe")
    me = lax.axis_index("mp")
    rows_in = section_in[0]
    images, length, width = rows_in.shape
    cols = out_weight.shape[1]
    heads = cols // HDIM
    hidden = fc1_weight.shape[2]
    hid = -(-hidden // HPAD) * HPAD
    chunks = -(-length // CHUNK)
    total = chunks * CHUNK
    hw = heads * HPAD
    scaling = HDIM ** (-0.5)
    rows_mp = lax.axis_size("mp") // 2
    piece = HALF // rows_mp
    pos = lax.rem(me, 2) * rows_mp + lax.div(me, 2)

    padded = jnp.pad(rows_in, ((0, 0), (0, total - length), (0, 0)))
    mine = lax.dynamic_index_in_dim(
        padded.reshape(images, chunks, 2 * rows_mp, piece, width), pos, 2, keepdims=False
    ).reshape(images, chunks * piece, width)

    def row_of(v):
        v = v.reshape(1, -1).astype(F32)
        return jnp.pad(v, ((0, 0), (0, width - v.shape[1])))

    vec = jnp.concatenate(
        [
            row_of(ln1_gain),
            row_of(ln1_bias),
            row_of(out_bias),
            row_of(ln2_gain),
            row_of(ln2_bias),
            row_of(fc1_bias),
            row_of(fc2_bias),
            jnp.zeros((1, width), F32),
        ]
    )
    lanes = ((0, 0), (0, 0), (0, 0), (0, HPAD - HDIM))
    tall = ((0, 0), (0, HPAD - HDIM), (0, 0))
    wqkv = jnp.transpose(qkv_weight[0], (1, 2, 0)).reshape(3 * heads, HDIM, width)
    wqkv = jnp.pad(wqkv, tall).reshape(3 * hw, width)
    bias_three = jnp.stack([qv_bias[0, 0], jnp.zeros_like(qv_bias[0, 0]), qv_bias[0, 1]])
    bqkv = jnp.pad(bias_three.reshape(1, 3, heads, HDIM), lanes).reshape(1, 3 * hw).astype(F32)
    wout = jnp.pad(out_weight[0].reshape(heads, HDIM, width), tall).reshape(hw, width)
    w1 = jnp.pad(fc1_weight[0].T, ((0, hid - hidden), (0, 0)))
    w2 = jnp.pad(fc2_weight[0], ((0, hid - hidden), (0, 0)))

    def arr(*shape, dtype=BF):
        return jax.ShapeDtypeStruct(shape, dtype)

    own = chunks * piece
    kept_shapes = [
        arr(images, own, width),
        arr(images, total, width),
        arr(images, total, 3 * hw),
        arr(images, total, hw),
        arr(images, total, HPAD, dtype=F32),
        arr(images, total, width),
        arr(images, total, hid),
        arr(images, total, hid),
        arr(images, own, width, dtype=F32),
    ]
    kept_vmem = [
        pltpu.VMEM((total, 3 * hw), BF),
        pltpu.VMEM((total, hw), BF),
        pltpu.VMEM((total, HPAD), F32),
        pltpu.VMEM((total, width), BF),
        pltpu.VMEM((total, hid), BF),
        pltpu.VMEM((total, hid), BF),
        pltpu.VMEM((own, width), F32),
    ]
    y_mine, *kept = pl.pallas_call(
        functools.partial(forward_kernel, images, chunks, heads, length, scaling, rows_mp),
        out_shape=[arr(images, own, width)] + kept_shapes,
        in_specs=[anywhere()] + [vmem()] * 6,
        out_specs=[anywhere()] * 10,
        scratch_shapes=[
            pltpu.VMEM((images, own, width), BF),
            pltpu.VMEM((2, total, width), BF),
            *kept_vmem,
            pltpu.VMEM((own, width), BF),
            *comm_scratch(chunks, width, rows_mp),
            *sems(images, chunks, rows_mp),
        ],
        compiler_params=pltpu.CompilerParams(
            collective_id=0, has_side_effects=True, vmem_limit_bytes=VMEM_LIMIT
        ),
        name="layer_forward",
    )(mine, vec, bqkv, wqkv, wout, w1, w2)

    dx_mine, gqkv, gout, g1, g2, small, gbqkv = pl.pallas_call(
        functools.partial(backward_kernel, images, chunks, heads, length, scaling, rows_mp),
        out_shape=[
            arr(images, own, width),
            arr(3 * hw, width, dtype=F32),
            arr(hw, width, dtype=F32),
            arr(hid, width, dtype=F32),
            arr(hid, width, dtype=F32),
            arr(8, width, dtype=F32),
            arr(1, 3 * hw, dtype=F32),
        ],
        in_specs=[anywhere()] + [vmem()] * 5 + [anywhere()] * 9,
        out_specs=[anywhere()] + [vmem()] * 6,
        scratch_shapes=[
            pltpu.VMEM((images, own, width), BF),
            pltpu.VMEM((own, width), BF),
            pltpu.VMEM((total, width), BF),
            *kept_vmem,
            pltpu.VMEM((total, width), BF),
            pltpu.VMEM((total, width), BF),
            pltpu.VMEM((total, 3 * hw), BF),
            pltpu.VMEM((total, 2 * hw), F32),
            pltpu.VMEM((CHUNK, hw), BF),
            pltpu.VMEM((own, width), BF),
            *comm_scratch(chunks, width, rows_mp),
            *sems(images, chunks, rows_mp),
        ],
        compiler_params=pltpu.CompilerParams(
            collective_id=1, has_side_effects=True, vmem_limit_bytes=VMEM_LIMIT
        ),
        name="layer_backward",
    )(mine, vec, wqkv, wout, w1, w2, *kept)

    out_mine = jnp.where(stage == 0, dx_mine, y_mine)
    whole = lax.all_gather(out_mine, "mp", axis=0)
    whole = whole.reshape(rows_mp, 2, images, chunks, piece, width)
    section_out = jnp.transpose(whole, (2, 3, 1, 0, 4, 5)).reshape(images, total, width)
    section_out = section_out[:, :length][None]

    gqkv = gqkv.reshape(3 * heads, HPAD, width)[:, :HDIM].reshape(3 * cols, width)
    gout = gout.reshape(heads, HPAD, width)[:, :HDIM].reshape(cols, width)
    stack = jnp.concatenate([g.astype(BF) for g in (gqkv, gout, g1[:hidden], g2[:hidden])])
    part = lax.psum_scatter(stack, "dp", scatter_dimension=1, tiled=True)
    stack = lax.all_gather(part, "dp", axis=1, tiled=True).astype(F32)
    gqkv, gout = stack[: 3 * cols], stack[3 * cols : 4 * cols]
    g1, g2 = stack[4 * cols : 4 * cols + hidden].T, stack[4 * cols + hidden :]
    gqkv = jnp.transpose(gqkv.reshape(3, cols, width), (2, 0, 1))
    gb = gbqkv.reshape(3, heads, HPAD)[:, :, :HDIM].reshape(3, cols)
    local = lax.psum((gb, small[5, :hidden]), "dp")
    wide = lax.psum(small, ("dp", "mp"))
    return (
        section_out,
        wide[0][None],
        wide[1][None],
        gqkv[None],
        jnp.stack([local[0][0], local[0][2]])[None],
        gout[None],
        wide[2][None],
        wide[3][None],
        wide[4][None],
        g1[None],
        local[1][None],
        g2[None],
        wide[6][None],
    )


def solution(mesh):
    vector, matrix = P("pipe", None), P("pipe", "mp", None)
    acts = P("pipe", "dp", None, None)
    heads = P("pipe", None, None, "mp")
    pair = P("pipe", None, "mp")
    params = (vector, vector, heads, pair, matrix, vector, vector, vector, pair, P("pipe", "mp"), matrix, vector)
    return jax.shard_map(
        on_device,
        mesh=mesh,
        in_specs=(acts, *params),
        out_specs=(acts, *params),
        check_vma=False,
    )
```

```python
import functools

import jax
import jax.numpy as jnp
from jax import lax
from jax.experimental import pallas as pl
from jax.experimental.pallas import tpu as pltpu
from jax.sharding import PartitionSpec as P

HDIM = 72
HPAD = 128
EPSILON = 1e-06
GELU_SCALE = 0.7978845608028654
GELU_CUBIC = 0.044715
MESH = pl.DeviceIdType.MESH
BF = jnp.bfloat16
F32 = jnp.float32
CHUNK = 256
HALF = CHUNK // 2
VMEM_LIMIT = 67043328
SKEW = 2
SLOTS = 4
PART_SLOTS = 8
SUM_SLOTS = 8


def dot_nn(a, b):
    return lax.dot_general(a, b, (((1,), (0,)), ((), ())), preferred_element_type=F32)


def dot_nt(a, b):
    return lax.dot_general(a, b, (((1,), (1,)), ((), ())), preferred_element_type=F32)


def dot_tn(a, b):
    return lax.dot_general(a, b, (((0,), (0,)), ((), ())), preferred_element_type=F32)


def col_sum(v):
    return jnp.sum(v, axis=0, keepdims=True)


def norm_stats(v):
    center = v - jnp.mean(v, axis=-1, keepdims=True)
    inv = lax.rsqrt(jnp.mean(center * center, axis=-1, keepdims=True) + EPSILON)
    return center * inv, inv


def norm_back(e, hat, inv, gain):
    d_hat = e * gain
    mean_d = jnp.mean(d_hat, axis=-1, keepdims=True)
    mean_dx = jnp.mean(d_hat * hat, axis=-1, keepdims=True)
    return inv * (d_hat - mean_d - hat * mean_dx)


class Spot:
    def __init__(self, rows):
        self.stage = lax.axis_index("pipe")
        me = lax.axis_index("mp")
        self.rows = rows
        self.core = lax.rem(me, 2)
        self.row = lax.div(me, 2)
        self.sib = self.row * 2 + (1 - self.core)
        self.piece = HALF // rows

    def ahead(self, j):
        return lax.rem(self.row + j, self.rows)

    def behind(self, j):
        return lax.rem(self.row + self.rows - j, self.rows)

    def peer(self, row):
        return {"mp": row * 2 + self.core}


def others(axis, count):
    me = lax.axis_index(axis)
    return [lax.rem(me + j, count) for j in range(1, count)]


def enter(spot, dp_n=1):
    barrier = pltpu.get_barrier_semaphore()
    targets = [{"pipe": 1 - spot.stage}]
    targets += [{"mp": t} for t in others("mp", 2 * spot.rows)]
    targets += [{"dp": t} for t in others("dp", dp_n)]
    for target in targets:
        pl.semaphore_signal(barrier, inc=1, device_id=target, device_id_type=MESH)
    pl.semaphore_wait(barrier, len(targets))


def remote(src, dst, send, recv, target):
    return pltpu.make_async_remote_copy(
        src_ref=src, dst_ref=dst, send_sem=send, recv_sem=recv, device_id=target, device_id_type=MESH
    )


class Gather:
    def __init__(self, buf, ssem, rsem, kind, spot):
        self.buf, self.ssem, self.rsem, self.kind, self.spot = buf, ssem, rsem, kind, spot

    def view(self, c, row):
        p = self.spot.piece
        start = c * CHUNK + self.spot.core * HALF + row * p
        return self.buf.at[pl.ds(pl.multiple_of(start, p), p)]

    def mine(self, c):
        return self.view(c, self.spot.row)

    def copy(self, c, which, view, target):
        k = self.kind + which
        return remote(view, view, self.ssem.at[k, c], self.rsem.at[k, c], target)

    def near_copy(self, c):
        return self.copy(c, 0, self.mine(c), {"mp": self.spot.sib})

    def far_copy(self, c, j):
        return self.copy(c, 2 * j - 1, self.mine(c), self.spot.peer(self.spot.ahead(j)))

    def pass_copy(self, c, j):
        return self.copy(c, 2 * j, self.view(c, self.spot.behind(j)), {"mp": self.spot.sib})

    def start(self, c):
        for j in range(1, self.spot.rows):
            self.far_copy(c, j).start()
        self.near_copy(c).start()

    def forward(self, c):
        for j in range(1, self.spot.rows):
            self.far_copy(c, j).wait_recv()
            self.pass_copy(c, j).start()

    def finish(self, c):
        self.near_copy(c).wait_recv()
        for j in range(1, self.spot.rows):
            self.pass_copy(c, j).wait_recv()

    def drain(self, c):
        self.near_copy(c).wait_send()
        for j in range(1, self.spot.rows):
            self.far_copy(c, j).wait_send()
            self.pass_copy(c, j).wait_send()


class Reduce:
    def __init__(self, part, near, out, far, ssem, rsem, kind, spot):
        self.part, self.near, self.out, self.far = part, near, out, far
        self.ssem, self.rsem, self.kind, self.spot = ssem, rsem, kind, spot

    def near_copy(self, c):
        src = self.part.at[c, pl.ds(pl.multiple_of((1 - self.spot.core) * HALF, HALF), HALF)]
        k = self.kind
        return remote(src, self.near.at[c], self.ssem.at[k, c], self.rsem.at[k, c], {"mp": self.spot.sib})

    def far_copy(self, c, j):
        k = self.kind + j
        target = self.spot.peer(self.spot.ahead(j))
        return remote(
            self.out.at[c, j - 1], self.far.at[c, j - 1], self.ssem.at[k, c], self.rsem.at[k, c], target
        )

    def start(self, c, value):
        self.part[c] = value.astype(BF)
        self.near_copy(c).start()

    def pair(self, c, row):
        p = self.spot.piece
        own = self.part[c, pl.ds(pl.multiple_of(self.spot.core * HALF + row * p, p), p)]
        near = self.near[c, pl.ds(pl.multiple_of(row * p, p), p)]
        return own.astype(F32) + near.astype(F32)

    def cross(self, c):
        self.near_copy(c).wait_recv()
        for j in range(1, self.spot.rows):
            self.out[c, j - 1] = self.pair(c, self.spot.ahead(j)).astype(BF)
            self.far_copy(c, j).start()

    def result(self, c):
        total = self.pair(c, self.spot.row)
        for j in range(1, self.spot.rows):
            self.far_copy(c, j).wait_recv()
            total = total + self.far[c, j - 1].astype(F32)
        return total

    def drain(self, c):
        self.near_copy(c).wait_send()
        for j in range(1, self.spot.rows):
            self.far_copy(c, j).wait_send()


def forward_kernel(
    images, chunks, heads, length, scaling, rows_mp,
    x_hbm, vec, bqkv, wqkv, wout, w1, w2,
    y_o, xin_o, a1_o, qkv_o, o_o, lse_o, a2_o, g_o, sl_o, h1_o,
    xbuf, a1b, qkvb, ob, lseb, a2b, gb, slb, h1b, outb,
    part1, near1, out1, far1, part2, near2, out2, far2,
    ssem, rsem, psend, precv, lsem,
):
    spot = Spot(rows_mp)
    stage, piece = spot.stage, spot.piece
    hw = heads * HPAD

    load = pltpu.make_async_copy(x_hbm, xbuf, lsem.at[0])

    @pl.when(stage == 0)
    def _():
        load.start()

    enter(spot)
    kinds = sem_kinds(rows_mp)
    gat2 = Gather(a2b, ssem, rsem, kinds[1], spot)
    red1 = Reduce(part1, near1, out1, far1, ssem, rsem, kinds[2], spot)
    red2 = Reduce(part2, near2, out2, far2, ssem, rsem, kinds[3], spot)

    def gat1(i):
        return Gather(a1b.at[lax.rem(i, 2)], ssem, rsem, kinds[0], spot)

    def vrow(r):
        return vec[r : r + 1, :]

    def pipe_copy(i, c):
        return remote(
            outb.at[pl.ds(c * piece, piece)],
            xbuf.at[i, pl.ds(c * piece, piece)],
            psend.at[c],
            precv.at[i, c],
            {"pipe": 1},
        )

    def y_copy(i, c):
        return pltpu.make_async_copy(
            outb.at[pl.ds(c * piece, piece)], y_o.at[i, pl.ds(c * piece, piece)], psend.at[c]
        )

    def begin(i, c):
        @pl.when(stage == 1)
        def _():
            pipe_copy(i, c).wait_recv()

        v = xbuf[i, pl.ds(c * piece, piece)].astype(F32)
        hat, _ = norm_stats(v)
        gat1(i).mine(c)[...] = (hat * vrow(0) + vrow(1)).astype(BF)
        gat1(i).start(c)

    def project(i, c):
        gat1(i).finish(c)
        a = a1b[lax.rem(i, 2), pl.ds(c * CHUNK, CHUNK)]
        qkvb[pl.ds(c * CHUNK, CHUNK)] = (dot_nt(a, wqkv[...]) + bqkv[...]).astype(BF)

    def attend(c):
        rows = pl.ds(c * CHUNK, CHUNK)
        total = chunks * CHUNK
        valid = lax.broadcasted_iota(jnp.int32, (CHUNK, total), 1) < length
        lane = lax.broadcasted_iota(jnp.int32, (CHUNK, HPAD), 1)
        kept = jnp.zeros((CHUNK, HPAD), F32)
        for h in range(heads):
            q = qkvb[rows, h * HPAD : (h + 1) * HPAD]
            k = qkvb[:, hw + h * HPAD : hw + (h + 1) * HPAD]
            v = qkvb[:, 2 * hw + h * HPAD : 2 * hw + (h + 1) * HPAD]
            s = jnp.where(valid, dot_nt(q, k) * scaling, -1e30)
            m = jnp.max(s, axis=-1, keepdims=True)
            e = jnp.exp(s - m)
            t = jnp.sum(e, axis=-1, keepdims=True)
            p = (e / t).astype(BF)
            ob[rows, h * HPAD : (h + 1) * HPAD] = dot_nn(p, v).astype(BF)
            kept = jnp.where(lane == h, m + jnp.log(t), kept)
        lseb[rows] = kept
        red1.start(c, dot_nn(ob[rows], wout[...]))

    def middle(i, c):
        sl = pl.ds(c * piece, piece)
        h1 = xbuf[i, sl].astype(F32) + red1.result(c) + vrow(2)
        h1b[sl] = h1
        hat, _ = norm_stats(h1)
        gat2.mine(c)[...] = (hat * vrow(3) + vrow(4)).astype(BF)
        gat2.start(c)

    def feed(c):
        rows = pl.ds(c * CHUNK, CHUNK)
        gat2.finish(c)
        u = dot_nt(a2b[rows], w1[...]) + vec[5:6, 0 : w1.shape[0]]
        uu = u * u
        t = jnp.tanh(GELU_SCALE * (u + GELU_CUBIC * uu * u))
        half = 0.5 * (1.0 + t)
        gb[rows] = (u * half).astype(BF)
        slb[rows] = (
            half + 0.5 * u * (1.0 - t * t) * (GELU_SCALE * (1.0 + 3.0 * GELU_CUBIC * uu))
        ).astype(BF)
        red2.start(c, dot_nn(gb[rows], w2[...]))

    def end(i, c):
        sl = pl.ds(c * piece, piece)
        outb[sl] = (h1b[sl] + red2.result(c) + vrow(6)).astype(BF)

        @pl.when(stage == 0)
        def _():
            pipe_copy(i, c).start()

        @pl.when(stage == 1)
        def _():
            y_copy(i, c).start()

    def end_wait(i, c):
        @pl.when(stage == 0)
        def _():
            pipe_copy(i, c).wait_send()

        @pl.when(stage == 1)
        def _():
            y_copy(i, c).wait()

    def saves(i):
        return [
            pltpu.make_async_copy(a, b, lsem.at[1 + n])
            for n, (a, b) in enumerate(
                (
                    (a1b.at[lax.rem(i, 2)], a1_o.at[i]),
                    (qkvb, qkv_o.at[i]),
                    (ob, o_o.at[i]),
                    (lseb, lse_o.at[i]),
                    (a2b, a2_o.at[i]),
                    (gb, g_o.at[i]),
                    (slb, sl_o.at[i]),
                    (h1b, h1_o.at[i]),
                    (xbuf.at[i], xin_o.at[i]),
                )
            )
        ]

    @pl.when(stage == 0)
    def _():
        load.wait()

    every = range(chunks)

    def first(i):
        for c in every:
            begin(i, c)

    def second(i):
        for c in every:
            gat1(i).forward(c)
        for c in every:
            project(i, c)
        for c in every:
            gat1(i).drain(c)

    first(0)
    second(0)

    def image(i, carry):
        sv = saves(i)
        sv[0].start()
        sv[1].start()
        for s in range(chunks + 6):
            def at(j):
                return s - j if 0 <= s - j < chunks else None

            c = at(0)
            if c is not None:
                attend(c)
            c = at(1)
            if c is not None:
                red1.cross(c)
            c = at(5)
            if c is not None:
                red2.cross(c)
            c = at(2)
            if c is not None:
                middle(i, c)
            c = at(3)
            if c is not None:
                gat2.forward(c)
            c = at(6)
            if c is not None:
                end(i, c)
            c = at(4)
            if c is not None:
                feed(c)
            if s == chunks:
                sv[2].start()
                sv[3].start()
        for n in range(4, 9):
            sv[n].start()
        for n in range(9):
            sv[n].wait()

        @pl.when(i + 1 < images)
        def _():
            first(i + 1)

        for c in every:
            red1.drain(c)
            red2.drain(c)
            gat2.drain(c)
            end_wait(i, c)

        @pl.when(i + 1 < images)
        def _():
            second(i + 1)

        return carry

    lax.fori_loop(0, images, image, 0)


def backward_kernel(
    images, chunks, heads, length, scaling, rows_mp, dp_n, pairs,
    d_hbm, y_in, vec, wqkv, wout, w1, w2,
    xin_i, a1_i, qkv_i, o_i, lse_i, a2_i, g_i, sl_i, h1_i,
    full_o, fin, sums_o,
    acc, small, gbqkv, obuf, fbuf, stage_buf, land_buf, sum_buf, mslot, dslot, sbuf, dbuf, xinb, a1b, qkvb, ob, lseb, a2b, gb, slb, h1b, dmb, dab, dqb, dkv, dob, outb,
    part1, near1, out1, far1,
    ssem, rsem, psend, precv, lsem, agsend, agrecv, msem, mrecv, dsem, drecv, zsend, zpart, zfinal, zpass, zkeep, pcredit, fcredit,
):
    spot = Spot(rows_mp)
    stage, piece = spot.stage, spot.piece
    hw = heads * HPAD
    hid = w1.shape[0]
    z = lax.axis_index("dp")
    me = lax.axis_index("mp")
    load = pltpu.make_async_copy(d_hbm, dbuf, lsem.at[0])
    load_y = pltpu.make_async_copy(y_in, obuf, lsem.at[10])

    @pl.when(stage == 1)
    def _():
        load.start()
        load_y.start()

    def loads(i):
        return [
            pltpu.make_async_copy(b, a, lsem.at[1 + n])
            for n, (a, b) in enumerate(
                (
                    (a1b, a1_i.at[i]),
                    (qkvb, qkv_i.at[i]),
                    (ob, o_i.at[i]),
                    (lseb, lse_i.at[i]),
                    (a2b, a2_i.at[i]),
                    (gb, g_i.at[i]),
                    (slb, sl_i.at[i]),
                    (h1b, h1_i.at[i]),
                    (xinb, xin_i.at[i]),
                )
            )
        ]

    for ld in loads(0):
        ld.start()
    enter(spot, dp_n)
    kinds = sem_kinds(rows_mp)
    gatm = Gather(dmb, ssem, rsem, kinds[0], spot)
    gata = Gather(dab, ssem, rsem, kinds[1], spot)
    red1 = Reduce(part1, near1, out1, far1, ssem, rsem, kinds[2], spot)
    red2 = Reduce(part1, near1, out1, far1, ssem, rsem, kinds[3], spot)
    every = range(chunks)

    acc[...] = jnp.zeros_like(acc)
    small[...] = jnp.zeros_like(small)
    gbqkv[...] = jnp.zeros_like(gbqkv)

    def add(r, v):
        small[r : r + 1, :] += v

    def pipe_copy(i, c):
        return remote(
            outb.at[pl.ds(c * piece, piece)],
            dbuf.at[i, pl.ds(c * piece, piece)],
            psend.at[c],
            precv.at[i, c],
            {"pipe": 0},
        )

    def begin(i, c):
        @pl.when(stage == 0)
        def _():
            pipe_copy(i, c).wait_recv()

        v = dbuf[i, pl.ds(c * piece, piece)]
        gatm.mine(c)[...] = v
        gatm.start(c)
        add(6, col_sum(v.astype(F32)))

    def feed(c):
        rows = pl.ds(c * CHUNK, CHUNK)
        gatm.finish(c)
        du = (dot_nt(dmb[rows], w2[...]) * slb[rows].astype(F32)).astype(BF)
        slb[rows] = du
        small[5:6, 0 : w1.shape[0]] += col_sum(du.astype(F32))
        red1.start(c, dot_nn(du, w1[...]))

    def middle(i, c):
        sl = pl.ds(c * piece, piece)
        e = red1.result(c)
        hat, inv = norm_stats(h1b[sl])
        add(3, col_sum(e * hat))
        add(4, col_sum(e))
        dh = dbuf[i, sl].astype(F32) + norm_back(e, hat, inv, vec[3:4, :])
        h1b[sl] = dh
        add(2, col_sum(dh))
        gata.mine(c)[...] = dh.astype(BF)
        gata.start(c)

    def weights(base, a, b, step):
        def tile(n, carry):
            cols = pl.ds(pl.multiple_of(n * step, step), step)
            acc[pl.ds(pl.multiple_of(base + n * step, step), step)] += dot_tn(a[:, cols], b[...])
            return carry

        lax.fori_loop(0, a.shape[1] // step, tile, 0)

    def attend(c):
        rows = pl.ds(c * CHUNK, CHUNK)
        total = chunks * CHUNK
        valid = lax.broadcasted_iota(jnp.int32, (CHUNK, total), 1) < length
        gata.finish(c)
        dob[...] = dot_nt(dab[rows], wout[...]).astype(BF)
        for h in range(heads):
            cq = slice(h * HPAD, (h + 1) * HPAD)
            ck = slice(hw + h * HPAD, hw + (h + 1) * HPAD)
            cv = slice(2 * hw + h * HPAD, 2 * hw + (h + 1) * HPAD)
            q, k, v = qkvb[rows, cq], qkvb[:, ck], qkvb[:, cv]
            d = dob[:, cq]
            s = dot_nt(q, k) * scaling
            p = jnp.where(valid, jnp.exp(s - lseb[rows, h : h + 1]), 0.0)
            dv = dot_tn(p.astype(BF), d)
            dp = dot_nt(d, v)
            inner = jnp.sum(dp * p, axis=-1, keepdims=True)
            ds = (p * (dp - inner)).astype(BF)
            dq = (dot_nn(ds, k) * scaling).astype(BF)
            dqb[rows, cq] = dq
            gbqkv[0:1, cq] += col_sum(dq.astype(F32))
            dk = dot_tn(ds, q)
            if c == 0:
                dkv[:, cq] = dk
                dkv[:, ck] = dv
            else:
                dkv[:, cq] += dk
                dkv[:, ck] += dv

    def close():
        dk = (dkv[:, 0:hw] * scaling).astype(BF)
        dqb[:, hw : 2 * hw] = dk
        dv = dkv[:, hw : 2 * hw].astype(BF)
        dqb[:, 2 * hw : 3 * hw] = dv
        gbqkv[0:1, 2 * hw : 3 * hw] += col_sum(dv.astype(F32))

    def unproject(c):
        rows = pl.ds(c * CHUNK, CHUNK)
        red2.start(c, dot_nn(dqb[rows], wqkv[...]))

    def end(i, c):
        sl = pl.ds(c * piece, piece)
        e = red2.result(c)
        hat, inv = norm_stats(xinb[sl].astype(F32))
        add(0, col_sum(e * hat))
        add(1, col_sum(e))
        dx = (h1b[sl] + norm_back(e, hat, inv, vec[0:1, :])).astype(BF)

        @pl.when(stage == 1)
        def _():
            outb[sl] = dx
            pipe_copy(i, c).start()

        @pl.when(stage == 0)
        def _():
            obuf[i, c] = dx

    def end_wait(i, c):
        @pl.when(stage == 1)
        def _():
            pipe_copy(i, c).wait_send()

    @pl.when(stage == 1)
    def _():
        load.wait()
        load_y.wait()

    def image(i, carry):
        ld = loads(i)
        for c in every:
            begin(i, c)
        for c in every:
            gatm.forward(c)
        for n in (5, 6):
            ld[n].wait()
        for c in every:
            feed(c)
            if c >= 1:
                red1.cross(c - 1)
        for n in (0, 1, 2, 3, 4, 7, 8):
            ld[n].wait()
        middle(i, 0)
        red1.cross(chunks - 1)
        for c in range(1, chunks - 1):
            middle(i, c)
        for c in every:
            gatm.drain(c)
        weights(0, gb, dmb, HPAD)
        middle(i, chunks - 1)
        for c in every:
            gata.forward(c)
        weights(hid, slb, a2b, HPAD)
        for c in every:
            attend(c)
        close()
        for c in every:
            red1.drain(c)
        for c in every:
            unproject(c)
            if c >= 1:
                red2.cross(c - 1)
        red2.cross(chunks - 1)
        for c in range(chunks - 1):
            end(i, c)
        weights(2 * hid, ob, dab, HPAD)
        end(i, chunks - 1)
        weights(2 * hid + hw, dqb, a1b, HPAD)
        for c in every:
            gata.drain(c)
            red2.drain(c)
            end_wait(i, c)

        @pl.when(i + 1 < images)
        def _():
            for nx in loads(i + 1):
                nx.start()

        return carry

    lax.fori_loop(0, images, image, 0)

    def block(core, row):
        return full_o.at[:, :, core * rows_mp + row]

    ag_own = pltpu.make_async_copy(obuf, block(spot.core, spot.row), lsem.at[0])

    def ag_near():
        return remote(obuf, block(spot.core, spot.row), agsend.at[0], agrecv.at[0], {"mp": spot.sib})

    def ag_far(j):
        k = 2 * j - 1
        return remote(obuf, fbuf.at[j - 1], agsend.at[k], agrecv.at[k], spot.peer(spot.ahead(j)))

    def ag_pass(j):
        view = block(spot.core, spot.behind(j))
        return remote(fbuf.at[j - 1], view, agsend.at[2 * j], agrecv.at[2 * j], {"mp": spot.sib})

    def ag_keep(j):
        return pltpu.make_async_copy(fbuf.at[j - 1], block(spot.core, spot.behind(j)), lsem.at[3 + j])

    ag_own.start()
    for j in range(1, rows_mp):
        ag_far(j).start()
    ag_near().start()

    mp_n = 2 * rows_mp

    def mp_copy(j):
        return remote(small, mslot.at[me], msem.at[j - 1], mrecv.at[j - 1], {"mp": lax.rem(me + j, mp_n)})

    def dp_copy(j):
        return remote(sbuf, dslot.at[z], dsem.at[j - 1], drecv.at[j - 1], {"dp": lax.rem(z + j, dp_n)})

    for j in range(1, mp_n):
        mp_copy(j).start()
    mslot[me] = small[...]
    for j in range(1, mp_n):
        mp_copy(j).wait_recv()
    total = mslot[0]
    for j in range(1, mp_n):
        total = total + mslot[j]
    own_row = lax.broadcasted_iota(jnp.int32, total.shape, 0) == 5
    sbuf[0:8] = jnp.where(own_row, small[...], total)
    sbuf[8:16] = jnp.zeros_like(total)
    sbuf[8:9, 0:hw] = gbqkv[0:1, 0:hw]
    sbuf[9:10, 0:hw] = gbqkv[0:1, 2 * hw : 3 * hw]
    for j in range(1, dp_n):
        dp_copy(j).start()
    dslot[z] = sbuf[...]

    tall = stage_buf.shape[1]
    units = fin.shape[0]
    wide_units = 2 * pairs
    right, left = lax.rem(z + 1, dp_n), lax.rem(z + dp_n - 1, dp_n)

    def owner(u):
        return dp_n // 2 - 1 + lax.rem(u, 2)

    def send_copy(dst, u, side, recv):
        slot = lax.rem(u, SLOTS)
        return remote(stage_buf.at[slot], dst, zsend.at[slot, side], recv, {"dp": left if side else right})

    def part_copy(u, side):
        slot = lax.rem(u, PART_SLOTS)
        return send_copy(land_buf.at[side, slot], u, side, zpart.at[side, slot])

    def sum_copy(u, side):
        slot = lax.rem(u, SUM_SLOTS)
        return send_copy(sum_buf.at[slot], u, side, zfinal.at[slot])

    def keep_copy(u):
        slot = lax.rem(u, SLOTS)
        return pltpu.make_async_copy(stage_buf.at[slot], fin.at[u], zsend.at[slot, 2])

    def pass_copy(u, side):
        slot = lax.rem(u, SUM_SLOTS)
        view = sum_buf.at[slot]
        return remote(view, view, zpass.at[slot], zfinal.at[slot], {"dp": left if side else right})

    def write_copy(u):
        slot = lax.rem(u, SUM_SLOTS)
        return pltpu.make_async_copy(sum_buf.at[slot], fin.at[u], zkeep.at[slot])

    def grant(sem, target):
        pl.semaphore_signal(sem, inc=1, device_id={"dp": target}, device_id_type=MESH)

    def sends(u, act):
        mid = owner(u)

        @pl.when((z <= mid) & (z < dp_n - 1))
        def _():
            act(0)

        @pl.when((z >= mid) & (z > 0))
        def _():
            act(1)

    def settle(u):
        sends(u, lambda side: part_copy(u, side).wait_send())

        @pl.when(z == owner(u))
        def _():
            keep_copy(u).wait()

    def start_sum(copy, u, side):
        @pl.when(u >= SUM_SLOTS)
        def _():
            pl.semaphore_wait(fcredit.at[side, lax.rem(u, 2)], 1)

        copy.start()

    def start_part(u, side):
        @pl.when(u >= PART_SLOTS)
        def _():
            pl.semaphore_wait(pcredit.at[side, lax.rem(u, 2)], 1)

        part_copy(u, side).start()

    def reduce_unit(u, value):
        mid = owner(u)
        from_left = (z > 0) & (z <= mid)
        from_right = (z < dp_n - 1) & (z >= mid)
        for side, cond in ((0, from_left), (1, from_right)):

            @pl.when(cond)
            def _(side=side):
                part_copy(u, side).wait_recv()

            value = value + jnp.where(cond, land_buf[side, lax.rem(u, PART_SLOTS)].astype(F32), 0.0)

        @pl.when(u >= SLOTS)
        def _():
            settle(u - SLOTS)

        stage_buf[lax.rem(u, SLOTS)] = value.astype(BF)
        for side, cond in ((0, from_left), (1, from_right)):

            @pl.when(cond & (u + PART_SLOTS < units))
            def _(side=side):
                grant(pcredit.at[side, lax.rem(u, 2)], right if side else left)

        @pl.when(z == mid)
        def _():
            keep_copy(u).start()
            sends(u, lambda side: start_sum(sum_copy(u, side), u, side))

        @pl.when(z != mid)
        def _():
            sends(u, lambda side: start_part(u, side))

    def release(u):
        mid = owner(u)
        write_copy(u).wait()

        @pl.when(((z < mid) & (z > 0)) | ((z > mid) & (z < dp_n - 1)))
        def _():
            pass_copy(u, 0).wait_send()

        @pl.when((z < mid) & (u + SUM_SLOTS < units))
        def _():
            grant(fcredit.at[1, lax.rem(u, 2)], right)

        @pl.when((z > mid) & (u + SUM_SLOTS < units))
        def _():
            grant(fcredit.at[0, lax.rem(u, 2)], left)

    def spread_unit(u):
        mid = owner(u)

        @pl.when(z != mid)
        def _():
            sum_copy(u, 0).wait_recv()
            write_copy(u).start()

            @pl.when((z < mid) & (z > 0))
            def _():
                start_sum(pass_copy(u, 1), u, 1)

            @pl.when((z > mid) & (z < dp_n - 1))
            def _():
                start_sum(pass_copy(u, 0), u, 0)

            @pl.when(u >= 2)
            def _():
                release(u - 2)

    half = dp_n // 2

    def unit(t, carry):
        mid = owner(t)
        late = t - SKEW * (half + jnp.abs(z - mid))
        now = t - SKEW * jnp.where(z < mid, z, jnp.where(z > mid, dp_n - 1 - z, half))

        @pl.when((z != mid) & (late >= 0) & (late < units))
        def _():
            spread_unit(late)

        @pl.when((now >= 0) & (now < wide_units))
        def _():
            start = now * tall + lax.div(now, pairs) * (hid - pairs * tall)
            reduce_unit(now, acc[pl.ds(pl.multiple_of(start, 8), tall)])

        @pl.when((now >= wide_units) & (now < units))
        def _():
            start = 2 * hid + (now - wide_units) * HPAD
            reduce_unit(now, acc[pl.ds(pl.multiple_of(start, HPAD), tall)])

        return carry

    lax.fori_loop(0, 8, unit, 0)
    for j in range(1, dp_n):
        dp_copy(j).wait_recv()
    total = dslot[0]
    for j in range(1, dp_n):
        total = total + dslot[j]
    sums_o[...] = total
    lax.fori_loop(8, 16, unit, 0)
    for j in range(1, rows_mp):
        ag_far(j).wait_recv()
        ag_pass(j).start()
        ag_keep(j).start()
    lax.fori_loop(16, units + SKEW * dp_n, unit, 0)

    def last(t, carry):
        settle(t)
        return carry

    lax.fori_loop(units - SLOTS, units, last, 0)

    def freed(u, carry):
        @pl.when(z != owner(u))
        def _():
            release(u)

        return carry

    lax.fori_loop(units - 2, units, freed, 0)
    ag_own.wait()
    ag_near().wait_send()
    ag_near().wait_recv()
    for j in range(1, rows_mp):
        ag_far(j).wait_send()
        ag_pass(j).wait_send()
        ag_pass(j).wait_recv()
        ag_keep(j).wait()
    for j in range(1, mp_n):
        mp_copy(j).wait_send()
    for j in range(1, dp_n):
        dp_copy(j).wait_send()


def vmem():
    return pl.BlockSpec(memory_space=pltpu.VMEM)


def anywhere():
    return pl.BlockSpec(memory_space=pl.ANY)


def comm_scratch(chunks, width, rows_mp):
    one = [
        pltpu.VMEM((chunks, CHUNK, width), BF),
        pltpu.VMEM((chunks, HALF, width), BF),
        pltpu.VMEM((chunks, rows_mp - 1, HALF // rows_mp, width), BF),
        pltpu.VMEM((chunks, rows_mp - 1, HALF // rows_mp, width), BF),
    ]
    return one + one


def sem_kinds(rows_mp):
    gather = 2 * rows_mp - 1
    return 0, gather, 2 * gather, 2 * gather + rows_mp


def sems(images, chunks, rows_mp):
    dma = pltpu.SemaphoreType.DMA
    kinds = 6 * rows_mp - 2
    return [dma((kinds, chunks)), dma((kinds, chunks)), dma((chunks,)), dma((images, chunks)), dma((11,))]


def on_device(
    section_in,
    ln1_gain,
    ln1_bias,
    qkv_weight,
    qv_bias,
    out_weight,
    out_bias,
    ln2_gain,
    ln2_bias,
    fc1_weight,
    fc1_bias,
    fc2_weight,
    fc2_bias,
):
    stage = lax.axis_index("pipe")
    me = lax.axis_index("mp")
    rows_in = section_in[0]
    images, length, width = rows_in.shape
    cols = out_weight.shape[1]
    heads = cols // HDIM
    hidden = fc1_weight.shape[2]
    hid = -(-hidden // HPAD) * HPAD
    chunks = -(-length // CHUNK)
    total = chunks * CHUNK
    hw = heads * HPAD
    scaling = HDIM ** (-0.5)
    rows_mp = lax.axis_size("mp") // 2
    piece = HALF // rows_mp
    pos = lax.rem(me, 2) * rows_mp + lax.div(me, 2)

    padded = jnp.pad(rows_in, ((0, 0), (0, total - length), (0, 0)))
    mine = lax.dynamic_index_in_dim(
        padded.reshape(images, chunks, 2 * rows_mp, piece, width), pos, 2, keepdims=False
    ).reshape(images, chunks * piece, width)

    def row_of(v):
        v = v.reshape(1, -1).astype(F32)
        return jnp.pad(v, ((0, 0), (0, width - v.shape[1])))

    vec = jnp.concatenate(
        [
            row_of(ln1_gain),
            row_of(ln1_bias),
            row_of(out_bias),
            row_of(ln2_gain),
            row_of(ln2_bias),
            row_of(fc1_bias),
            row_of(fc2_bias),
            jnp.zeros((1, width), F32),
        ]
    )
    lanes = ((0, 0), (0, 0), (0, 0), (0, HPAD - HDIM))
    tall = ((0, 0), (0, HPAD - HDIM), (0, 0))
    wqkv = jnp.transpose(qkv_weight[0], (1, 2, 0)).reshape(3 * heads, HDIM, width)
    wqkv = jnp.pad(wqkv, tall).reshape(3 * hw, width)
    bias_three = jnp.stack([qv_bias[0, 0], jnp.zeros_like(qv_bias[0, 0]), qv_bias[0, 1]])
    bqkv = jnp.pad(bias_three.reshape(1, 3, heads, HDIM), lanes).reshape(1, 3 * hw).astype(F32)
    wout = jnp.pad(out_weight[0].reshape(heads, HDIM, width), tall).reshape(hw, width)
    w1 = jnp.pad(fc1_weight[0].T, ((0, hid - hidden), (0, 0)))
    w2 = jnp.pad(fc2_weight[0], ((0, hid - hidden), (0, 0)))

    def arr(*shape, dtype=BF):
        return jax.ShapeDtypeStruct(shape, dtype)

    own = chunks * piece
    kept_shapes = [
        arr(images, own, width),
        arr(images, total, width),
        arr(images, total, 3 * hw),
        arr(images, total, hw),
        arr(images, total, HPAD, dtype=F32),
        arr(images, total, width),
        arr(images, total, hid),
        arr(images, total, hid),
        arr(images, own, width, dtype=F32),
    ]
    kept_vmem = [
        pltpu.VMEM((total, 3 * hw), BF),
        pltpu.VMEM((total, hw), BF),
        pltpu.VMEM((total, HPAD), F32),
        pltpu.VMEM((total, width), BF),
        pltpu.VMEM((total, hid), BF),
        pltpu.VMEM((total, hid), BF),
        pltpu.VMEM((own, width), F32),
    ]
    y_mine, *kept = pl.pallas_call(
        functools.partial(forward_kernel, images, chunks, heads, length, scaling, rows_mp),
        out_shape=[arr(images, own, width)] + kept_shapes,
        in_specs=[anywhere()] + [vmem()] * 6,
        out_specs=[anywhere()] * 10,
        scratch_shapes=[
            pltpu.VMEM((images, own, width), BF),
            pltpu.VMEM((2, total, width), BF),
            *kept_vmem,
            pltpu.VMEM((own, width), BF),
            *comm_scratch(chunks, width, rows_mp),
            *sems(images, chunks, rows_mp),
        ],
        compiler_params=pltpu.CompilerParams(
            collective_id=0, has_side_effects=True, vmem_limit_bytes=VMEM_LIMIT
        ),
        name="layer_forward",
    )(mine, vec, bqkv, wqkv, wout, w1, w2)

    dp_n = lax.axis_size("dp")
    tall_unit = HDIM
    pairs = -(-hidden // tall_unit)
    units = 2 * pairs + 4 * heads
    dma = pltpu.SemaphoreType.DMA
    full, fin, sums = pl.pallas_call(
        functools.partial(backward_kernel, images, chunks, heads, length, scaling, rows_mp, dp_n, pairs),
        out_shape=[
            arr(images, chunks, 2 * rows_mp, piece, width),
            arr(units, tall_unit, width),
            arr(16, width, dtype=F32),
        ],
        in_specs=[anywhere()] * 2 + [vmem()] * 5 + [anywhere()] * 9,
        out_specs=[anywhere()] * 2 + [vmem()],
        scratch_shapes=[
            pltpu.VMEM((2 * hid + 4 * hw, width), F32),
            pltpu.VMEM((8, width), F32),
            pltpu.VMEM((1, 3 * hw), F32),
            pltpu.VMEM((images, chunks, piece, width), BF),
            pltpu.VMEM((rows_mp - 1, images, chunks, piece, width), BF),
            pltpu.VMEM((SLOTS, tall_unit, width), BF),
            pltpu.VMEM((2, PART_SLOTS, tall_unit, width), BF),
            pltpu.VMEM((SUM_SLOTS, tall_unit, width), BF),
            pltpu.VMEM((2 * rows_mp, 8, width), F32),
            pltpu.VMEM((dp_n, 16, width), F32),
            pltpu.VMEM((16, width), F32),
            pltpu.VMEM((images, own, width), BF),
            pltpu.VMEM((own, width), BF),
            pltpu.VMEM((total, width), BF),
            *kept_vmem,
            pltpu.VMEM((total, width), BF),
            pltpu.VMEM((total, width), BF),
            pltpu.VMEM((total, 3 * hw), BF),
            pltpu.VMEM((total, 2 * hw), F32),
            pltpu.VMEM((CHUNK, hw), BF),
            pltpu.VMEM((own, width), BF),
            *comm_scratch(chunks, width, rows_mp)[:4],
            *sems(images, chunks, rows_mp),
            dma((2 * rows_mp - 1,)),
            dma((2 * rows_mp - 1,)),
            dma((2 * rows_mp - 1,)),
            dma((2 * rows_mp - 1,)),
            dma((dp_n - 1,)),
            dma((dp_n - 1,)),
            dma((SLOTS, 3)),
            dma((2, PART_SLOTS)),
            dma((SUM_SLOTS,)),
            dma((SUM_SLOTS,)),
            dma((SUM_SLOTS,)),
            pltpu.SemaphoreType.REGULAR((2, 2)),
            pltpu.SemaphoreType.REGULAR((2, 2)),
        ],
        compiler_params=pltpu.CompilerParams(
            collective_id=1, has_side_effects=True, vmem_limit_bytes=VMEM_LIMIT
        ),
        name="layer_backward",
    )(mine, y_mine.reshape(images, chunks, piece, width), vec, wqkv, wout, w1, w2, *kept)

    section_out = full.reshape(images, total, width)[:, :length][None]
    rows = fin.reshape(units * tall_unit, width)

    def take(start, count):
        return rows[start : start + count].astype(F32)

    base = 2 * pairs * tall_unit
    g2, g1 = take(0, hidden), take(pairs * tall_unit, hidden).T
    gout, gqkv = take(base, cols), take(base + cols, 3 * cols)
    gqkv = jnp.transpose(gqkv.reshape(3, cols, width), (2, 0, 1))
    gb = sums[8:10, :hw].reshape(2, heads, HPAD)[:, :, :HDIM].reshape(1, 2, cols)
    return (
        section_out,
        sums[0:1],
        sums[1:2],
        gqkv[None],
        gb,
        gout[None],
        sums[2:3],
        sums[3:4],
        sums[4:5],
        g1[None],
        sums[5:6, :hidden],
        g2[None],
        sums[6:7],
    )


def solution(mesh):
    vector, matrix = P("pipe", None), P("pipe", "mp", None)
    acts = P("pipe", "dp", None, None)
    heads = P("pipe", None, None, "mp")
    pair = P("pipe", None, "mp")
    params = (vector, vector, heads, pair, matrix, vector, vector, vector, pair, P("pipe", "mp"), matrix, vector)
    return jax.shard_map(
        on_device,
        mesh=mesh,
        in_specs=(acts, *params),
        out_specs=(acts, *params),
        check_vma=False,
    )
```

```python
import functools

import jax
import jax.numpy as jnp
from jax import lax
from jax.experimental import pallas as pl
from jax.experimental.pallas import tpu as pltpu
from jax.sharding import PartitionSpec as P

HDIM = 72
HPAD = 128
EPSILON = 1e-06
GELU_SCALE = 0.7978845608028654
GELU_CUBIC = 0.044715
MESH = pl.DeviceIdType.MESH
BF = jnp.bfloat16
F32 = jnp.float32
CHUNK = 256
HALF = CHUNK // 2
VMEM_LIMIT = 67043328
SKEW = 2
AHEAD = 16
SLOTS = 4
PART_SLOTS = 8
SUM_SLOTS = 8


def dot_nn(a, b):
    return lax.dot_general(a, b, (((1,), (0,)), ((), ())), preferred_element_type=F32)


def dot_nt(a, b):
    return lax.dot_general(a, b, (((1,), (1,)), ((), ())), preferred_element_type=F32)


def dot_tn(a, b):
    return lax.dot_general(a, b, (((0,), (0,)), ((), ())), preferred_element_type=F32)


def col_sum(v):
    return jnp.sum(v, axis=0, keepdims=True)


def norm_stats(v):
    center = v - jnp.mean(v, axis=-1, keepdims=True)
    inv = lax.rsqrt(jnp.mean(center * center, axis=-1, keepdims=True) + EPSILON)
    return center * inv, inv


def norm_back(e, hat, inv, gain):
    d_hat = e * gain
    mean_d = jnp.mean(d_hat, axis=-1, keepdims=True)
    mean_dx = jnp.mean(d_hat * hat, axis=-1, keepdims=True)
    return inv * (d_hat - mean_d - hat * mean_dx)


class Spot:
    def __init__(self, rows):
        self.stage = lax.axis_index("pipe")
        me = lax.axis_index("mp")
        self.rows = rows
        self.core = lax.rem(me, 2)
        self.row = lax.div(me, 2)
        self.sib = self.row * 2 + (1 - self.core)
        self.piece = HALF // rows

    def ahead(self, j):
        return lax.rem(self.row + j, self.rows)

    def behind(self, j):
        return lax.rem(self.row + self.rows - j, self.rows)

    def peer(self, row):
        return {"mp": row * 2 + self.core}


def others(axis, count):
    me = lax.axis_index(axis)
    return [lax.rem(me + j, count) for j in range(1, count)]


def enter(spot, dp_n=1):
    barrier = pltpu.get_barrier_semaphore()
    targets = [{"pipe": 1 - spot.stage}]
    targets += [{"mp": t} for t in others("mp", 2 * spot.rows)]
    targets += [{"dp": t} for t in others("dp", dp_n)]
    for target in targets:
        pl.semaphore_signal(barrier, inc=1, device_id=target, device_id_type=MESH)
    pl.semaphore_wait(barrier, len(targets))


def remote(src, dst, send, recv, target):
    return pltpu.make_async_remote_copy(
        src_ref=src, dst_ref=dst, send_sem=send, recv_sem=recv, device_id=target, device_id_type=MESH
    )


class Gather:
    def __init__(self, buf, ssem, rsem, kind, spot):
        self.buf, self.ssem, self.rsem, self.kind, self.spot = buf, ssem, rsem, kind, spot

    def view(self, c, row):
        p = self.spot.piece
        start = c * CHUNK + self.spot.core * HALF + row * p
        return self.buf.at[pl.ds(pl.multiple_of(start, p), p)]

    def mine(self, c):
        return self.view(c, self.spot.row)

    def copy(self, c, which, view, target):
        k = self.kind + which
        return remote(view, view, self.ssem.at[k, c], self.rsem.at[k, c], target)

    def near_copy(self, c):
        return self.copy(c, 0, self.mine(c), {"mp": self.spot.sib})

    def far_copy(self, c, j):
        return self.copy(c, 2 * j - 1, self.mine(c), self.spot.peer(self.spot.ahead(j)))

    def pass_copy(self, c, j):
        return self.copy(c, 2 * j, self.view(c, self.spot.behind(j)), {"mp": self.spot.sib})

    def start(self, c):
        for j in range(1, self.spot.rows):
            self.far_copy(c, j).start()
        self.near_copy(c).start()

    def forward(self, c):
        for j in range(1, self.spot.rows):
            self.far_copy(c, j).wait_recv()
            self.pass_copy(c, j).start()

    def finish(self, c):
        self.near_copy(c).wait_recv()
        for j in range(1, self.spot.rows):
            self.pass_copy(c, j).wait_recv()

    def drain(self, c):
        self.near_copy(c).wait_send()
        for j in range(1, self.spot.rows):
            self.far_copy(c, j).wait_send()
            self.pass_copy(c, j).wait_send()


class Reduce:
    def __init__(self, part, near, out, far, ssem, rsem, kind, spot):
        self.part, self.near, self.out, self.far = part, near, out, far
        self.ssem, self.rsem, self.kind, self.spot = ssem, rsem, kind, spot

    def near_copy(self, c):
        src = self.part.at[c, pl.ds(pl.multiple_of((1 - self.spot.core) * HALF, HALF), HALF)]
        k = self.kind
        return remote(src, self.near.at[c], self.ssem.at[k, c], self.rsem.at[k, c], {"mp": self.spot.sib})

    def far_copy(self, c, j):
        k = self.kind + j
        target = self.spot.peer(self.spot.ahead(j))
        return remote(
            self.out.at[c, j - 1], self.far.at[c, j - 1], self.ssem.at[k, c], self.rsem.at[k, c], target
        )

    def start(self, c, value):
        self.part[c] = value.astype(BF)
        self.near_copy(c).start()

    def pair(self, c, row):
        p = self.spot.piece
        own = self.part[c, pl.ds(pl.multiple_of(self.spot.core * HALF + row * p, p), p)]
        near = self.near[c, pl.ds(pl.multiple_of(row * p, p), p)]
        return own.astype(F32) + near.astype(F32)

    def cross(self, c):
        self.near_copy(c).wait_recv()
        for j in range(1, self.spot.rows):
            self.out[c, j - 1] = self.pair(c, self.spot.ahead(j)).astype(BF)
            self.far_copy(c, j).start()

    def result(self, c):
        total = self.pair(c, self.spot.row)
        for j in range(1, self.spot.rows):
            self.far_copy(c, j).wait_recv()
            total = total + self.far[c, j - 1].astype(F32)
        return total

    def drain(self, c):
        self.near_copy(c).wait_send()
        for j in range(1, self.spot.rows):
            self.far_copy(c, j).wait_send()


def forward_kernel(
    images, chunks, heads, length, scaling, rows_mp,
    x_hbm, vec, bqkv, wqkv, wout, w1, w2,
    y_o, xin_o, a1_o, qkv_o, o_o, lse_o, a2_o, g_o, sl_o, h1_o,
    xbuf, a1b, qkvb, ob, lseb, a2b, gb, slb, h1b, outb,
    part1, near1, out1, far1, part2, near2, out2, far2,
    ssem, rsem, psend, precv, lsem,
):
    spot = Spot(rows_mp)
    stage, piece = spot.stage, spot.piece
    hw = heads * HPAD

    load = pltpu.make_async_copy(x_hbm, xbuf, lsem.at[0])

    @pl.when(stage == 0)
    def _():
        load.start()

    enter(spot)
    kinds = sem_kinds(rows_mp)
    gat2 = Gather(a2b, ssem, rsem, kinds[1], spot)
    red1 = Reduce(part1, near1, out1, far1, ssem, rsem, kinds[2], spot)
    red2 = Reduce(part2, near2, out2, far2, ssem, rsem, kinds[3], spot)

    def gat1(i):
        return Gather(a1b.at[lax.rem(i, 2)], ssem, rsem, kinds[0], spot)

    def vrow(r):
        return vec[r : r + 1, :]

    def pipe_copy(i, c):
        return remote(
            outb.at[pl.ds(c * piece, piece)],
            xbuf.at[i, pl.ds(c * piece, piece)],
            psend.at[c],
            precv.at[i, c],
            {"pipe": 1},
        )

    def y_copy(i, c):
        return pltpu.make_async_copy(
            outb.at[pl.ds(c * piece, piece)], y_o.at[i, pl.ds(c * piece, piece)], psend.at[c]
        )

    def begin(i, c):
        @pl.when(stage == 1)
        def _():
            pipe_copy(i, c).wait_recv()

        v = xbuf[i, pl.ds(c * piece, piece)].astype(F32)
        hat, _ = norm_stats(v)
        gat1(i).mine(c)[...] = (hat * vrow(0) + vrow(1)).astype(BF)
        gat1(i).start(c)

    def project(i, c):
        gat1(i).finish(c)
        a = a1b[lax.rem(i, 2), pl.ds(c * CHUNK, CHUNK)]
        qkvb[pl.ds(c * CHUNK, CHUNK)] = (dot_nt(a, wqkv[...]) + bqkv[...]).astype(BF)

    def attend(c):
        rows = pl.ds(c * CHUNK, CHUNK)
        total = chunks * CHUNK
        valid = lax.broadcasted_iota(jnp.int32, (CHUNK, total), 1) < length
        lane = lax.broadcasted_iota(jnp.int32, (CHUNK, HPAD), 1)
        kept = jnp.zeros((CHUNK, HPAD), F32)
        for h in range(heads):
            q = qkvb[rows, h * HPAD : (h + 1) * HPAD]
            k = qkvb[:, hw + h * HPAD : hw + (h + 1) * HPAD]
            v = qkvb[:, 2 * hw + h * HPAD : 2 * hw + (h + 1) * HPAD]
            s = jnp.where(valid, dot_nt(q, k) * scaling, -1e30)
            m = jnp.max(s, axis=-1, keepdims=True)
            e = jnp.exp(s - m)
            t = jnp.sum(e, axis=-1, keepdims=True)
            p = (e / t).astype(BF)
            ob[rows, h * HPAD : (h + 1) * HPAD] = dot_nn(p, v).astype(BF)
            kept = jnp.where(lane == h, m + jnp.log(t), kept)
        lseb[rows] = kept
        red1.start(c, dot_nn(ob[rows], wout[...]))

    def middle(i, c):
        sl = pl.ds(c * piece, piece)
        h1 = xbuf[i, sl].astype(F32) + red1.result(c) + vrow(2)
        h1b[sl] = h1
        hat, _ = norm_stats(h1)
        gat2.mine(c)[...] = (hat * vrow(3) + vrow(4)).astype(BF)
        gat2.start(c)

    def feed(c):
        rows = pl.ds(c * CHUNK, CHUNK)
        gat2.finish(c)
        u = dot_nt(a2b[rows], w1[...]) + vec[5:6, 0 : w1.shape[0]]
        uu = u * u
        t = jnp.tanh(GELU_SCALE * (u + GELU_CUBIC * uu * u))
        half = 0.5 * (1.0 + t)
        gb[rows] = (u * half).astype(BF)
        slb[rows] = (
            half + 0.5 * u * (1.0 - t * t) * (GELU_SCALE * (1.0 + 3.0 * GELU_CUBIC * uu))
        ).astype(BF)
        red2.start(c, dot_nn(gb[rows], w2[...]))

    def end(i, c):
        sl = pl.ds(c * piece, piece)
        outb[sl] = (h1b[sl] + red2.result(c) + vrow(6)).astype(BF)

        @pl.when(stage == 0)
        def _():
            pipe_copy(i, c).start()

        @pl.when(stage == 1)
        def _():
            y_copy(i, c).start()

    def end_wait(i, c):
        @pl.when(stage == 0)
        def _():
            pipe_copy(i, c).wait_send()

        @pl.when(stage == 1)
        def _():
            y_copy(i, c).wait()

    def saves(i):
        return [
            pltpu.make_async_copy(a, b, lsem.at[1 + n])
            for n, (a, b) in enumerate(
                (
                    (a1b.at[lax.rem(i, 2)], a1_o.at[i]),
                    (qkvb, qkv_o.at[i]),
                    (ob, o_o.at[i]),
                    (lseb, lse_o.at[i]),
                    (a2b, a2_o.at[i]),
                    (gb, g_o.at[i]),
                    (slb, sl_o.at[i]),
                    (h1b, h1_o.at[i]),
                    (xbuf.at[i], xin_o.at[i]),
                )
            )
        ]

    @pl.when(stage == 0)
    def _():
        load.wait()

    every = range(chunks)

    def first(i):
        for c in every:
            begin(i, c)

    def second(i):
        for c in every:
            gat1(i).forward(c)
        for c in every:
            project(i, c)
        for c in every:
            gat1(i).drain(c)

    first(0)
    second(0)

    def image(i, carry):
        sv = saves(i)
        sv[0].start()
        sv[1].start()
        for s in range(chunks + 6):
            def at(j):
                return s - j if 0 <= s - j < chunks else None

            c = at(0)
            if c is not None:
                attend(c)
            c = at(1)
            if c is not None:
                red1.cross(c)
            c = at(5)
            if c is not None:
                red2.cross(c)
            c = at(2)
            if c is not None:
                middle(i, c)
            c = at(3)
            if c is not None:
                gat2.forward(c)
            c = at(6)
            if c is not None:
                end(i, c)
            c = at(4)
            if c is not None:
                feed(c)
            if s == chunks:
                sv[2].start()
                sv[3].start()
        for n in range(4, 9):
            sv[n].start()
        for n in range(9):
            sv[n].wait()

        @pl.when(i + 1 < images)
        def _():
            first(i + 1)

        for c in every:
            red1.drain(c)
            red2.drain(c)
            gat2.drain(c)
            end_wait(i, c)

        @pl.when(i + 1 < images)
        def _():
            second(i + 1)

        return carry

    lax.fori_loop(0, images, image, 0)


def backward_kernel(
    images, chunks, heads, length, scaling, rows_mp, dp_n, pairs,
    d_hbm, y_in, vec, wqkv, wout, w1, w2,
    xin_i, a1_i, qkv_i, o_i, lse_i, a2_i, g_i, sl_i, h1_i,
    full_o, fin, sums_o,
    acc, small, gbqkv, obuf, fbuf, stage_buf, land_buf, sum_buf, mslot, dslot, sbuf, dbuf, xinb, a1b, qkvb, ob, lseb, a2b, gb, slb, h1b, dmb, dab, dqb, dkv, dob, outb,
    part1, near1, out1, far1, part2, near2, out2, far2,
    ssem, rsem, psend, precv, lsem, agsend, agrecv, msem, mrecv, dsem, drecv, zsend, zpart, zfinal, zpass, zkeep, pcredit, fcredit,
):
    spot = Spot(rows_mp)
    stage, piece = spot.stage, spot.piece
    hw = heads * HPAD
    hid = w1.shape[0]
    z = lax.axis_index("dp")
    me = lax.axis_index("mp")
    load = pltpu.make_async_copy(d_hbm, dbuf, lsem.at[0])
    load_y = pltpu.make_async_copy(y_in, obuf, lsem.at[10])

    @pl.when(stage == 1)
    def _():
        load.start()
        load_y.start()

    def loads(i):
        return [
            pltpu.make_async_copy(b, a, lsem.at[1 + n])
            for n, (a, b) in enumerate(
                (
                    (a1b, a1_i.at[i]),
                    (qkvb, qkv_i.at[i]),
                    (ob, o_i.at[i]),
                    (lseb, lse_i.at[i]),
                    (a2b, a2_i.at[i]),
                    (gb, g_i.at[i]),
                    (slb, sl_i.at[i]),
                    (h1b, h1_i.at[i]),
                    (xinb, xin_i.at[i]),
                )
            )
        ]

    back_loads, front_loads = (7, 1, 2, 3, 0, 8), (4, 5, 6)
    for n in back_loads:
        loads(0)[n].start()
    enter(spot, dp_n)
    kinds = sem_kinds(rows_mp)
    gatm = Gather(dmb, ssem, rsem, kinds[0], spot)
    gata = Gather(dab, ssem, rsem, kinds[1], spot)
    red1 = Reduce(part1, near1, out1, far1, ssem, rsem, kinds[2], spot)
    red2 = Reduce(part2, near2, out2, far2, ssem, rsem, kinds[3], spot)
    every = range(chunks)

    acc[...] = jnp.zeros_like(acc)
    small[...] = jnp.zeros_like(small)
    gbqkv[...] = jnp.zeros_like(gbqkv)

    def add(r, v):
        small[r : r + 1, :] += v

    def pipe_copy(i, c):
        return remote(
            outb.at[pl.ds(c * piece, piece)],
            dbuf.at[i, pl.ds(c * piece, piece)],
            psend.at[c],
            precv.at[i, c],
            {"pipe": 0},
        )

    def begin(i, c):
        @pl.when(stage == 0)
        def _():
            pipe_copy(i, c).wait_recv()

        v = dbuf[i, pl.ds(c * piece, piece)]
        gatm.mine(c)[...] = v
        gatm.start(c)
        add(6, col_sum(v.astype(F32)))

    def feed(c):
        rows = pl.ds(c * CHUNK, CHUNK)
        gatm.finish(c)
        du = (dot_nt(dmb[rows], w2[...]) * slb[rows].astype(F32)).astype(BF)
        slb[rows] = du
        small[5:6, 0 : w1.shape[0]] += col_sum(du.astype(F32))
        red1.start(c, dot_nn(du, w1[...]))

    def middle(i, c):
        sl = pl.ds(c * piece, piece)
        e = red1.result(c)
        hat, inv = norm_stats(h1b[sl])
        add(3, col_sum(e * hat))
        add(4, col_sum(e))
        dh = dbuf[i, sl].astype(F32) + norm_back(e, hat, inv, vec[3:4, :])
        h1b[sl] = dh
        add(2, col_sum(dh))
        gata.mine(c)[...] = dh.astype(BF)
        gata.start(c)

    def weights(base, a, b, step):
        def tile(n, carry):
            cols = pl.ds(pl.multiple_of(n * step, step), step)
            acc[pl.ds(pl.multiple_of(base + n * step, step), step)] += dot_tn(a[:, cols], b[...])
            return carry

        lax.fori_loop(0, a.shape[1] // step, tile, 0)

    def head_weights(base, a, b):
        def head(n, carry):
            cols = pl.ds(pl.multiple_of(n * HPAD, HPAD), HPAD)
            start = base + n * HDIM
            acc[pl.ds(pl.multiple_of(start, 8), HDIM)] += dot_tn(a[:, cols], b[...])[:HDIM]
            return carry

        lax.fori_loop(0, a.shape[1] // HPAD, head, 0)

    def attend(c, between=()):
        rows = pl.ds(c * CHUNK, CHUNK)
        total = chunks * CHUNK
        valid = lax.broadcasted_iota(jnp.int32, (CHUNK, total), 1) < length
        gata.finish(c)
        dob[...] = dot_nt(dab[rows], wout[...]).astype(BF)
        for h in range(heads):
            cq = slice(h * HPAD, (h + 1) * HPAD)
            ck = slice(hw + h * HPAD, hw + (h + 1) * HPAD)
            cv = slice(2 * hw + h * HPAD, 2 * hw + (h + 1) * HPAD)
            q, k, v = qkvb[rows, cq], qkvb[:, ck], qkvb[:, cv]
            d = dob[:, cq]
            s = dot_nt(q, k) * scaling
            p = jnp.where(valid, jnp.exp(s - lseb[rows, h : h + 1]), 0.0)
            dv = dot_tn(p.astype(BF), d)
            dp = dot_nt(d, v)
            inner = jnp.sum(dp * p, axis=-1, keepdims=True)
            ds = (p * (dp - inner)).astype(BF)
            dq = (dot_nn(ds, k) * scaling).astype(BF)
            dqb[rows, cq] = dq
            gbqkv[0:1, cq] += col_sum(dq.astype(F32))
            dk = dot_tn(ds, q)
            if c == 0:
                dkv[:, cq] = dk
                dkv[:, ck] = dv
            else:
                dkv[:, cq] += dk
                dkv[:, ck] += dv
            if h == heads // 2 - 1:
                for action in between:
                    action()

    def close():
        dk = (dkv[:, 0:hw] * scaling).astype(BF)
        dqb[:, hw : 2 * hw] = dk
        dv = dkv[:, hw : 2 * hw].astype(BF)
        dqb[:, 2 * hw : 3 * hw] = dv
        gbqkv[0:1, 2 * hw : 3 * hw] += col_sum(dv.astype(F32))

    def unproject(c):
        rows = pl.ds(c * CHUNK, CHUNK)
        red2.start(c, dot_nn(dqb[rows], wqkv[...]))

    def end(i, c):
        sl = pl.ds(c * piece, piece)
        e = red2.result(c)
        hat, inv = norm_stats(xinb[sl].astype(F32))
        add(0, col_sum(e * hat))
        add(1, col_sum(e))
        dx = (h1b[sl] + norm_back(e, hat, inv, vec[0:1, :])).astype(BF)

        @pl.when(stage == 1)
        def _():
            outb[sl] = dx
            pipe_copy(i, c).start()

        @pl.when(stage == 0)
        def _():
            obuf[i, c] = dx

    def end_wait(i, c):
        @pl.when(stage == 1)
        def _():
            pipe_copy(i, c).wait_send()

    @pl.when(stage == 1)
    def _():
        load.wait()
        load_y.wait()

    tall = stage_buf.shape[1]
    units = fin.shape[0]
    wide_units = 2 * pairs
    right, left = lax.rem(z + 1, dp_n), lax.rem(z + dp_n - 1, dp_n)

    def owner(u):
        return dp_n // 2 - 1 + lax.rem(u, 2)

    def send_copy(dst, u, side, recv):
        slot = lax.rem(u, SLOTS)
        return remote(stage_buf.at[slot], dst, zsend.at[slot, side], recv, {"dp": left if side else right})

    def part_copy(u, side):
        slot = lax.rem(u, PART_SLOTS)
        return send_copy(land_buf.at[side, slot], u, side, zpart.at[side, slot])

    def sum_copy(u, side):
        slot = lax.rem(u, SUM_SLOTS)
        return send_copy(sum_buf.at[slot], u, side, zfinal.at[slot])

    def keep_copy(u):
        slot = lax.rem(u, SLOTS)
        return pltpu.make_async_copy(stage_buf.at[slot], fin.at[u], zsend.at[slot, 2])

    def pass_copy(u, side):
        slot = lax.rem(u, SUM_SLOTS)
        view = sum_buf.at[slot]
        return remote(view, view, zpass.at[slot], zfinal.at[slot], {"dp": left if side else right})

    def write_copy(u):
        slot = lax.rem(u, SUM_SLOTS)
        return pltpu.make_async_copy(sum_buf.at[slot], fin.at[u], zkeep.at[slot])

    def grant(sem, target):
        pl.semaphore_signal(sem, inc=1, device_id={"dp": target}, device_id_type=MESH)

    def sends(u, act):
        mid = owner(u)

        @pl.when((z <= mid) & (z < dp_n - 1))
        def _():
            act(0)

        @pl.when((z >= mid) & (z > 0))
        def _():
            act(1)

    def settle(u):
        sends(u, lambda side: part_copy(u, side).wait_send())

        @pl.when(z == owner(u))
        def _():
            keep_copy(u).wait()

    def start_sum(copy, u, side):
        @pl.when(u >= SUM_SLOTS)
        def _():
            pl.semaphore_wait(fcredit.at[side, lax.rem(u, 2)], 1)

        copy.start()

    def start_part(u, side):
        @pl.when(u >= PART_SLOTS)
        def _():
            pl.semaphore_wait(pcredit.at[side, lax.rem(u, 2)], 1)

        part_copy(u, side).start()

    def reduce_unit(u, value):
        mid = owner(u)
        from_left = (z > 0) & (z <= mid)
        from_right = (z < dp_n - 1) & (z >= mid)
        for side, cond in ((0, from_left), (1, from_right)):

            @pl.when(cond)
            def _(side=side):
                part_copy(u, side).wait_recv()

            value = value + jnp.where(cond, land_buf[side, lax.rem(u, PART_SLOTS)].astype(F32), 0.0)

        @pl.when(u >= SLOTS)
        def _():
            settle(u - SLOTS)

        stage_buf[lax.rem(u, SLOTS)] = value.astype(BF)
        for side, cond in ((0, from_left), (1, from_right)):

            @pl.when(cond & (u + PART_SLOTS < units))
            def _(side=side):
                grant(pcredit.at[side, lax.rem(u, 2)], right if side else left)

        @pl.when(z == mid)
        def _():
            keep_copy(u).start()
            sends(u, lambda side: start_sum(sum_copy(u, side), u, side))

        @pl.when(z != mid)
        def _():
            sends(u, lambda side: start_part(u, side))

    def release(u):
        mid = owner(u)
        write_copy(u).wait()

        @pl.when(((z < mid) & (z > 0)) | ((z > mid) & (z < dp_n - 1)))
        def _():
            pass_copy(u, 0).wait_send()

        @pl.when((z < mid) & (u + SUM_SLOTS < units))
        def _():
            grant(fcredit.at[1, lax.rem(u, 2)], right)

        @pl.when((z > mid) & (u + SUM_SLOTS < units))
        def _():
            grant(fcredit.at[0, lax.rem(u, 2)], left)

    def spread_unit(u):
        mid = owner(u)

        @pl.when(z != mid)
        def _():
            sum_copy(u, 0).wait_recv()
            write_copy(u).start()

            @pl.when((z < mid) & (z > 0))
            def _():
                start_sum(pass_copy(u, 1), u, 1)

            @pl.when((z > mid) & (z < dp_n - 1))
            def _():
                start_sum(pass_copy(u, 0), u, 0)

            @pl.when(u >= 2)
            def _():
                release(u - 2)

    half = dp_n // 2

    def unit(t, carry):
        mid = owner(t)
        late = t - SKEW * (half + jnp.abs(z - mid))
        now = t - SKEW * jnp.where(z < mid, z, jnp.where(z > mid, dp_n - 1 - z, half))

        @pl.when((z != mid) & (late >= 0) & (late < units))
        def _():
            spread_unit(late)

        @pl.when((now >= 0) & (now < wide_units))
        def _():
            start = now * tall + lax.div(now, pairs) * (hid - pairs * tall)
            reduce_unit(now, acc[pl.ds(pl.multiple_of(start, 8), tall)])

        @pl.when((now >= wide_units) & (now < units))
        def _():
            start = 2 * hid + (now - wide_units) * tall
            reduce_unit(now, acc[pl.ds(pl.multiple_of(start, 8), tall)])

        return carry

    def slot(s, carry):
        b, f = s - 1, s
        has_b, has_f = b >= 0, f < images
        back, front = pl.when(has_b), pl.when(has_f)
        early, late = pl.when(has_f & (stage == 1)), pl.when(has_f & (stage == 0))

        def chain(lo, hi):
            @pl.when(b == images - 1)
            def _():
                lax.fori_loop(lo, hi, unit, 0)

        @back
        def _():
            loads(b)[7].wait()
            for c in every:
                middle(b, c)
            for c in every:
                red1.drain(c)
            weights(hid, slb, a2b, HPAD)

        chain(0, 2)

        @front
        def _():
            for n in front_loads:
                loads(f)[n].start()

        @back
        def _():
            for n in (0, 1, 2, 3, 8):
                loads(b)[n].wait()
            gata.forward(0)
            attend(0, [functools.partial(gata.forward, c) for c in range(1, chunks - 1)])

        @early
        def _():
            for c in every:
                begin(f, c)

        def pass_early():
            @early
            def _():
                for c in range(chunks - 1):
                    gatm.forward(c)

        chain(2, 5)

        @back
        def _():
            gata.forward(chunks - 1)
            for c in range(1, chunks - 1):
                attend(c)

        chain(5, 8)

        @back
        def _():
            attend(chunks - 1, [pass_early])

        @pl.when(has_f & jnp.logical_not(has_b))
        def _():
            pass_early()

        chain(8, 11)

        @back
        def _():
            close()
            for c in range(chunks - 1):
                unproject(c)
                if c >= 1:
                    red2.cross(c - 1)
            head_weights(2 * hid, ob, dab)
            for c in every:
                gata.drain(c)
            unproject(chunks - 1)
            red2.cross(chunks - 2)

        @late
        def _():
            for c in every:
                begin(f, c)
            for c in range(chunks - 1):
                gatm.forward(c)

        @front
        def _():
            gatm.forward(chunks - 1)
            for n in front_loads:
                loads(f)[n].wait()

        chain(11, 14)
        for c in every:

            @front
            def _():
                feed(c)

            @back
            def _():
                if c == 0:
                    red2.cross(chunks - 1)
                end(b, c)

            @front
            def _():
                red1.cross(c)

        @pl.when(has_b & (b + 1 < images))
        def _():
            loads(b + 1)[back_loads[0]].start()

        @front
        def _():
            for c in every:
                gatm.drain(c)
            weights(0, gb, dmb, HPAD)

        chain(14, AHEAD)

        @back
        def _():
            head_weights(2 * hid + heads * HDIM, dqb, a1b)
            for c in every:
                red2.drain(c)
                end_wait(b, c)

        @pl.when(has_b & (b + 1 < images))
        def _():
            for n in back_loads[1:]:
                loads(b + 1)[n].start()

        return carry

    lax.fori_loop(0, images + 1, slot, 0)

    def block(core, row):
        return full_o.at[:, :, core * rows_mp + row]

    ag_own = pltpu.make_async_copy(obuf, block(spot.core, spot.row), lsem.at[0])

    def ag_near():
        return remote(obuf, block(spot.core, spot.row), agsend.at[0], agrecv.at[0], {"mp": spot.sib})

    def ag_far(j):
        k = 2 * j - 1
        return remote(obuf, fbuf.at[j - 1], agsend.at[k], agrecv.at[k], spot.peer(spot.ahead(j)))

    def ag_pass(j):
        view = block(spot.core, spot.behind(j))
        return remote(fbuf.at[j - 1], view, agsend.at[2 * j], agrecv.at[2 * j], {"mp": spot.sib})

    def ag_keep(j):
        return pltpu.make_async_copy(fbuf.at[j - 1], block(spot.core, spot.behind(j)), lsem.at[3 + j])

    ag_own.start()
    for j in range(1, rows_mp):
        ag_far(j).start()
    ag_near().start()

    mp_n = 2 * rows_mp

    def mp_copy(j):
        return remote(small, mslot.at[me], msem.at[j - 1], mrecv.at[j - 1], {"mp": lax.rem(me + j, mp_n)})

    def dp_copy(j):
        return remote(sbuf, dslot.at[z], dsem.at[j - 1], drecv.at[j - 1], {"dp": lax.rem(z + j, dp_n)})

    for j in range(1, mp_n):
        mp_copy(j).start()
    mslot[me] = small[...]
    for j in range(1, mp_n):
        mp_copy(j).wait_recv()
    total = mslot[0]
    for j in range(1, mp_n):
        total = total + mslot[j]
    own_row = lax.broadcasted_iota(jnp.int32, total.shape, 0) == 5
    sbuf[0:8] = jnp.where(own_row, small[...], total)
    sbuf[8:16] = jnp.zeros_like(total)
    sbuf[8:9, 0:hw] = gbqkv[0:1, 0:hw]
    sbuf[9:10, 0:hw] = gbqkv[0:1, 2 * hw : 3 * hw]
    for j in range(1, dp_n):
        dp_copy(j).start()
    dslot[z] = sbuf[...]

    for j in range(1, dp_n):
        dp_copy(j).wait_recv()
    total = dslot[0]
    for j in range(1, dp_n):
        total = total + dslot[j]
    sums_o[...] = total
    lax.fori_loop(AHEAD, AHEAD + 4, unit, 0)
    for j in range(1, rows_mp):
        ag_far(j).wait_recv()
        ag_pass(j).start()
        ag_keep(j).start()
    lax.fori_loop(AHEAD + 4, units + SKEW * dp_n, unit, 0)

    def last(t, carry):
        settle(t)
        return carry

    lax.fori_loop(units - SLOTS, units, last, 0)

    def freed(u, carry):
        @pl.when(z != owner(u))
        def _():
            release(u)

        return carry

    lax.fori_loop(units - 2, units, freed, 0)
    ag_own.wait()
    ag_near().wait_send()
    ag_near().wait_recv()
    for j in range(1, rows_mp):
        ag_far(j).wait_send()
        ag_pass(j).wait_send()
        ag_pass(j).wait_recv()
        ag_keep(j).wait()
    for j in range(1, mp_n):
        mp_copy(j).wait_send()
    for j in range(1, dp_n):
        dp_copy(j).wait_send()


def vmem():
    return pl.BlockSpec(memory_space=pltpu.VMEM)


def anywhere():
    return pl.BlockSpec(memory_space=pl.ANY)


def comm_scratch(chunks, width, rows_mp):
    one = [
        pltpu.VMEM((chunks, CHUNK, width), BF),
        pltpu.VMEM((chunks, HALF, width), BF),
        pltpu.VMEM((chunks, rows_mp - 1, HALF // rows_mp, width), BF),
        pltpu.VMEM((chunks, rows_mp - 1, HALF // rows_mp, width), BF),
    ]
    return one + one


def sem_kinds(rows_mp):
    gather = 2 * rows_mp - 1
    return 0, gather, 2 * gather, 2 * gather + rows_mp


def sems(images, chunks, rows_mp):
    dma = pltpu.SemaphoreType.DMA
    kinds = 6 * rows_mp - 2
    return [dma((kinds, chunks)), dma((kinds, chunks)), dma((chunks,)), dma((images, chunks)), dma((11,))]


def on_device(
    section_in,
    ln1_gain,
    ln1_bias,
    qkv_weight,
    qv_bias,
    out_weight,
    out_bias,
    ln2_gain,
    ln2_bias,
    fc1_weight,
    fc1_bias,
    fc2_weight,
    fc2_bias,
):
    stage = lax.axis_index("pipe")
    me = lax.axis_index("mp")
    rows_in = section_in[0]
    images, length, width = rows_in.shape
    cols = out_weight.shape[1]
    heads = cols // HDIM
    hidden = fc1_weight.shape[2]
    hid = -(-hidden // HPAD) * HPAD
    chunks = -(-length // CHUNK)
    total = chunks * CHUNK
    hw = heads * HPAD
    scaling = HDIM ** (-0.5)
    rows_mp = lax.axis_size("mp") // 2
    piece = HALF // rows_mp
    pos = lax.rem(me, 2) * rows_mp + lax.div(me, 2)

    padded = jnp.pad(rows_in, ((0, 0), (0, total - length), (0, 0)))
    mine = lax.dynamic_index_in_dim(
        padded.reshape(images, chunks, 2 * rows_mp, piece, width), pos, 2, keepdims=False
    ).reshape(images, chunks * piece, width)

    def row_of(v):
        v = v.reshape(1, -1).astype(F32)
        return jnp.pad(v, ((0, 0), (0, width - v.shape[1])))

    vec = jnp.concatenate(
        [
            row_of(ln1_gain),
            row_of(ln1_bias),
            row_of(out_bias),
            row_of(ln2_gain),
            row_of(ln2_bias),
            row_of(fc1_bias),
            row_of(fc2_bias),
            jnp.zeros((1, width), F32),
        ]
    )
    lanes = ((0, 0), (0, 0), (0, 0), (0, HPAD - HDIM))
    tall = ((0, 0), (0, HPAD - HDIM), (0, 0))
    wqkv = jnp.transpose(qkv_weight[0], (1, 2, 0)).reshape(3 * heads, HDIM, width)
    wqkv = jnp.pad(wqkv, tall).reshape(3 * hw, width)
    bias_three = jnp.stack([qv_bias[0, 0], jnp.zeros_like(qv_bias[0, 0]), qv_bias[0, 1]])
    bqkv = jnp.pad(bias_three.reshape(1, 3, heads, HDIM), lanes).reshape(1, 3 * hw).astype(F32)
    wout = jnp.pad(out_weight[0].reshape(heads, HDIM, width), tall).reshape(hw, width)
    w1 = jnp.pad(fc1_weight[0].T, ((0, hid - hidden), (0, 0)))
    w2 = jnp.pad(fc2_weight[0], ((0, hid - hidden), (0, 0)))

    def arr(*shape, dtype=BF):
        return jax.ShapeDtypeStruct(shape, dtype)

    own = chunks * piece
    kept_shapes = [
        arr(images, own, width),
        arr(images, total, width),
        arr(images, total, 3 * hw),
        arr(images, total, hw),
        arr(images, total, HPAD, dtype=F32),
        arr(images, total, width),
        arr(images, total, hid),
        arr(images, total, hid),
        arr(images, own, width, dtype=F32),
    ]
    kept_vmem = [
        pltpu.VMEM((total, 3 * hw), BF),
        pltpu.VMEM((total, hw), BF),
        pltpu.VMEM((total, HPAD), F32),
        pltpu.VMEM((total, width), BF),
        pltpu.VMEM((total, hid), BF),
        pltpu.VMEM((total, hid), BF),
        pltpu.VMEM((own, width), F32),
    ]
    y_mine, *kept = pl.pallas_call(
        functools.partial(forward_kernel, images, chunks, heads, length, scaling, rows_mp),
        out_shape=[arr(images, own, width)] + kept_shapes,
        in_specs=[anywhere()] + [vmem()] * 6,
        out_specs=[anywhere()] * 10,
        scratch_shapes=[
            pltpu.VMEM((images, own, width), BF),
            pltpu.VMEM((2, total, width), BF),
            *kept_vmem,
            pltpu.VMEM((own, width), BF),
            *comm_scratch(chunks, width, rows_mp),
            *sems(images, chunks, rows_mp),
        ],
        compiler_params=pltpu.CompilerParams(
            collective_id=0, has_side_effects=True, vmem_limit_bytes=VMEM_LIMIT
        ),
        name="layer_forward",
    )(mine, vec, bqkv, wqkv, wout, w1, w2)

    dp_n = lax.axis_size("dp")
    tall_unit = HDIM
    pairs = -(-hidden // tall_unit)
    units = 2 * pairs + 4 * heads
    dma = pltpu.SemaphoreType.DMA
    full, fin, sums = pl.pallas_call(
        functools.partial(backward_kernel, images, chunks, heads, length, scaling, rows_mp, dp_n, pairs),
        out_shape=[
            arr(images, chunks, 2 * rows_mp, piece, width),
            arr(units, tall_unit, width),
            arr(16, width, dtype=F32),
        ],
        in_specs=[anywhere()] * 2 + [vmem()] * 5 + [anywhere()] * 9,
        out_specs=[anywhere()] * 2 + [vmem()],
        scratch_shapes=[
            pltpu.VMEM((2 * hid + 4 * cols, width), F32),
            pltpu.VMEM((8, width), F32),
            pltpu.VMEM((1, 3 * hw), F32),
            pltpu.VMEM((images, chunks, piece, width), BF),
            pltpu.VMEM((rows_mp - 1, images, chunks, piece, width), BF),
            pltpu.VMEM((SLOTS, tall_unit, width), BF),
            pltpu.VMEM((2, PART_SLOTS, tall_unit, width), BF),
            pltpu.VMEM((SUM_SLOTS, tall_unit, width), BF),
            pltpu.VMEM((2 * rows_mp, 8, width), F32),
            pltpu.VMEM((dp_n, 16, width), F32),
            pltpu.VMEM((16, width), F32),
            pltpu.VMEM((images, own, width), BF),
            pltpu.VMEM((own, width), BF),
            pltpu.VMEM((total, width), BF),
            *kept_vmem,
            pltpu.VMEM((total, width), BF),
            pltpu.VMEM((total, width), BF),
            pltpu.VMEM((total, 3 * hw), BF),
            pltpu.VMEM((total, 2 * hw), F32),
            pltpu.VMEM((CHUNK, hw), BF),
            pltpu.VMEM((own, width), BF),
            *comm_scratch(chunks, width, rows_mp),
            *sems(images, chunks, rows_mp),
            dma((2 * rows_mp - 1,)),
            dma((2 * rows_mp - 1,)),
            dma((2 * rows_mp - 1,)),
            dma((2 * rows_mp - 1,)),
            dma((dp_n - 1,)),
            dma((dp_n - 1,)),
            dma((SLOTS, 3)),
            dma((2, PART_SLOTS)),
            dma((SUM_SLOTS,)),
            dma((SUM_SLOTS,)),
            dma((SUM_SLOTS,)),
            pltpu.SemaphoreType.REGULAR((2, 2)),
            pltpu.SemaphoreType.REGULAR((2, 2)),
        ],
        compiler_params=pltpu.CompilerParams(
            collective_id=1, has_side_effects=True, vmem_limit_bytes=VMEM_LIMIT
        ),
        name="layer_backward",
    )(mine, y_mine.reshape(images, chunks, piece, width), vec, wqkv, wout, w1, w2, *kept)

    section_out = full.reshape(images, total, width)[:, :length][None]
    rows = fin.reshape(units * tall_unit, width)

    def take(start, count):
        return rows[start : start + count].astype(F32)

    base = 2 * pairs * tall_unit
    g2, g1 = take(0, hidden), take(pairs * tall_unit, hidden).T
    gout, gqkv = take(base, cols), take(base + cols, 3 * cols)
    gqkv = jnp.transpose(gqkv.reshape(3, cols, width), (2, 0, 1))
    gb = sums[8:10, :hw].reshape(2, heads, HPAD)[:, :, :HDIM].reshape(1, 2, cols)
    return (
        section_out,
        sums[0:1],
        sums[1:2],
        gqkv[None],
        gb,
        gout[None],
        sums[2:3],
        sums[3:4],
        sums[4:5],
        g1[None],
        sums[5:6, :hidden],
        g2[None],
        sums[6:7],
    )


def solution(mesh):
    vector, matrix = P("pipe", None), P("pipe", "mp", None)
    acts = P("pipe", "dp", None, None)
    heads = P("pipe", None, None, "mp")
    pair = P("pipe", None, "mp")
    params = (vector, vector, heads, pair, matrix, vector, vector, vector, pair, P("pipe", "mp"), matrix, vector)
    return jax.shard_map(
        on_device,
        mesh=mesh,
        in_specs=(acts, *params),
        out_specs=(acts, *params),
        check_vma=False,
    )
```

```python
import functools

import jax
import jax.numpy as jnp
from jax import lax
from jax.experimental import pallas as pl
from jax.experimental.pallas import tpu as pltpu
from jax.sharding import PartitionSpec as P

HDIM = 72
HPAD = 128
EPSILON = 1e-06
GELU_SCALE = 0.7978845608028654
GELU_CUBIC = 0.044715
MESH = pl.DeviceIdType.MESH
BF = jnp.bfloat16
F32 = jnp.float32
CHUNK = 256
HALF = CHUNK // 2
VMEM_LIMIT = 67043328
SKEW = 2
AHEAD = 16
SLOTS = 4
PART_SLOTS = 8
SUM_SLOTS = 8


def dot_nn(a, b):
    return lax.dot_general(a, b, (((1,), (0,)), ((), ())), preferred_element_type=F32)


def dot_nt(a, b):
    return lax.dot_general(a, b, (((1,), (1,)), ((), ())), preferred_element_type=F32)


def dot_tn(a, b):
    return lax.dot_general(a, b, (((0,), (0,)), ((), ())), preferred_element_type=F32)


def tile_of(size):
    return next(t for t in (512, 384, 256, HPAD) if size % t == 0)


def col_sum(v):
    return jnp.sum(v, axis=0, keepdims=True)


def norm_stats(v):
    center = v - jnp.mean(v, axis=-1, keepdims=True)
    inv = lax.rsqrt(jnp.mean(center * center, axis=-1, keepdims=True) + EPSILON)
    return center * inv, inv


def norm_back(e, hat, inv, gain):
    d_hat = e * gain
    mean_d = jnp.mean(d_hat, axis=-1, keepdims=True)
    mean_dx = jnp.mean(d_hat * hat, axis=-1, keepdims=True)
    return inv * (d_hat - mean_d - hat * mean_dx)


class Spot:
    def __init__(self, rows):
        self.stage = lax.axis_index("pipe")
        me = lax.axis_index("mp")
        self.rows = rows
        self.core = lax.rem(me, 2)
        self.row = lax.div(me, 2)
        self.sib = self.row * 2 + (1 - self.core)
        self.piece = HALF // rows

    def ahead(self, j):
        return lax.rem(self.row + j, self.rows)

    def behind(self, j):
        return lax.rem(self.row + self.rows - j, self.rows)

    def peer(self, row):
        return {"mp": row * 2 + self.core}


def others(axis, count):
    me = lax.axis_index(axis)
    return [lax.rem(me + j, count) for j in range(1, count)]


def enter(spot, dp_n=1):
    barrier = pltpu.get_barrier_semaphore()
    targets = [{"pipe": 1 - spot.stage}]
    targets += [{"mp": t} for t in others("mp", 2 * spot.rows)]
    targets += [{"dp": t} for t in others("dp", dp_n)]
    for target in targets:
        pl.semaphore_signal(barrier, inc=1, device_id=target, device_id_type=MESH)
    pl.semaphore_wait(barrier, len(targets))


def remote(src, dst, send, recv, target):
    return pltpu.make_async_remote_copy(
        src_ref=src, dst_ref=dst, send_sem=send, recv_sem=recv, device_id=target, device_id_type=MESH
    )


class Gather:
    def __init__(self, buf, ssem, rsem, kind, spot):
        self.buf, self.ssem, self.rsem, self.kind, self.spot = buf, ssem, rsem, kind, spot

    def view(self, c, row):
        p = self.spot.piece
        start = c * CHUNK + self.spot.core * HALF + row * p
        return self.buf.at[pl.ds(pl.multiple_of(start, p), p)]

    def mine(self, c):
        return self.view(c, self.spot.row)

    def copy(self, c, which, view, target):
        k = self.kind + which
        return remote(view, view, self.ssem.at[k, c], self.rsem.at[k, c], target)

    def near_copy(self, c):
        return self.copy(c, 0, self.mine(c), {"mp": self.spot.sib})

    def far_copy(self, c, j):
        return self.copy(c, 2 * j - 1, self.mine(c), self.spot.peer(self.spot.ahead(j)))

    def pass_copy(self, c, j):
        return self.copy(c, 2 * j, self.view(c, self.spot.behind(j)), {"mp": self.spot.sib})

    def start(self, c):
        for j in range(1, self.spot.rows):
            self.far_copy(c, j).start()
        self.near_copy(c).start()

    def forward(self, c):
        for j in range(1, self.spot.rows):
            self.far_copy(c, j).wait_recv()
            self.pass_copy(c, j).start()

    def finish(self, c):
        self.near_copy(c).wait_recv()
        for j in range(1, self.spot.rows):
            self.pass_copy(c, j).wait_recv()

    def drain(self, c):
        self.near_copy(c).wait_send()
        for j in range(1, self.spot.rows):
            self.far_copy(c, j).wait_send()
            self.pass_copy(c, j).wait_send()


class Reduce:
    def __init__(self, part, near, out, far, ssem, rsem, kind, spot):
        self.part, self.near, self.out, self.far = part, near, out, far
        self.ssem, self.rsem, self.kind, self.spot = ssem, rsem, kind, spot

    def near_copy(self, c):
        src = self.part.at[c, pl.ds(pl.multiple_of((1 - self.spot.core) * HALF, HALF), HALF)]
        k = self.kind
        return remote(src, self.near.at[c], self.ssem.at[k, c], self.rsem.at[k, c], {"mp": self.spot.sib})

    def far_copy(self, c, j):
        k = self.kind + j
        target = self.spot.peer(self.spot.ahead(j))
        return remote(
            self.out.at[c, j - 1], self.far.at[c, j - 1], self.ssem.at[k, c], self.rsem.at[k, c], target
        )

    def start(self, c, value):
        self.part[c] = value.astype(BF)
        self.near_copy(c).start()

    def pair(self, c, row):
        p = self.spot.piece
        own = self.part[c, pl.ds(pl.multiple_of(self.spot.core * HALF + row * p, p), p)]
        near = self.near[c, pl.ds(pl.multiple_of(row * p, p), p)]
        return own.astype(F32) + near.astype(F32)

    def cross(self, c):
        self.near_copy(c).wait_recv()
        for j in range(1, self.spot.rows):
            self.out[c, j - 1] = self.pair(c, self.spot.ahead(j)).astype(BF)
            self.far_copy(c, j).start()

    def result(self, c):
        total = self.pair(c, self.spot.row)
        for j in range(1, self.spot.rows):
            self.far_copy(c, j).wait_recv()
            total = total + self.far[c, j - 1].astype(F32)
        return total

    def drain(self, c):
        self.near_copy(c).wait_send()
        for j in range(1, self.spot.rows):
            self.far_copy(c, j).wait_send()


def forward_kernel(
    images, chunks, heads, length, scaling, rows_mp,
    x_hbm, vec, bqkv, wqkv, wout, w1, w2,
    y_o, xin_o, a1_o, qkv_o, o_o, lse_o, a2_o, g_o, sl_o, h1_o,
    xbuf, a1b, qkvb, ob, lseb, a2b, gb, slb, h1b, outb,
    part1, near1, out1, far1, part2, near2, out2, far2,
    ssem, rsem, psend, precv, lsem,
):
    spot = Spot(rows_mp)
    stage, piece = spot.stage, spot.piece
    hw = heads * HPAD

    load = pltpu.make_async_copy(x_hbm, xbuf, lsem.at[0])

    @pl.when(stage == 0)
    def _():
        load.start()

    enter(spot)
    kinds = sem_kinds(rows_mp)
    gat2 = Gather(a2b, ssem, rsem, kinds[1], spot)
    red1 = Reduce(part1, near1, out1, far1, ssem, rsem, kinds[2], spot)
    red2 = Reduce(part2, near2, out2, far2, ssem, rsem, kinds[3], spot)

    def gat1(i):
        return Gather(a1b.at[lax.rem(i, 2)], ssem, rsem, kinds[0], spot)

    def vrow(r):
        return vec[r : r + 1, :]

    def pipe_copy(i, c):
        return remote(
            outb.at[pl.ds(c * piece, piece)],
            xbuf.at[i, pl.ds(c * piece, piece)],
            psend.at[c],
            precv.at[i, c],
            {"pipe": 1},
        )

    def y_copy(i, c):
        return pltpu.make_async_copy(
            outb.at[pl.ds(c * piece, piece)], y_o.at[i, pl.ds(c * piece, piece)], psend.at[c]
        )

    def begin(i, c):
        @pl.when(stage == 1)
        def _():
            pipe_copy(i, c).wait_recv()

        v = xbuf[i, pl.ds(c * piece, piece)].astype(F32)
        hat, _ = norm_stats(v)
        gat1(i).mine(c)[...] = (hat * vrow(0) + vrow(1)).astype(BF)
        gat1(i).start(c)

    def project(i, c):
        gat1(i).finish(c)
        a = a1b[lax.rem(i, 2), pl.ds(c * CHUNK, CHUNK)]
        qkvb[pl.ds(c * CHUNK, CHUNK)] = (dot_nt(a, wqkv[...]) + bqkv[...]).astype(BF)

    def attend(c):
        rows = pl.ds(c * CHUNK, CHUNK)
        total = chunks * CHUNK
        valid = lax.broadcasted_iota(jnp.int32, (CHUNK, total), 1) < length
        lane = lax.broadcasted_iota(jnp.int32, (CHUNK, HPAD), 1)
        kept = jnp.zeros((CHUNK, HPAD), F32)
        for h in range(heads):
            q = qkvb[rows, h * HPAD : (h + 1) * HPAD]
            k = qkvb[:, hw + h * HPAD : hw + (h + 1) * HPAD]
            v = qkvb[:, 2 * hw + h * HPAD : 2 * hw + (h + 1) * HPAD]
            s = jnp.where(valid, dot_nt(q, k) * scaling, -1e30)
            m = jnp.max(s, axis=-1, keepdims=True)
            e = jnp.exp(s - m)
            t = jnp.sum(e, axis=-1, keepdims=True)
            p = (e / t).astype(BF)
            ob[rows, h * HPAD : (h + 1) * HPAD] = dot_nn(p, v).astype(BF)
            kept = jnp.where(lane == h, m + jnp.log(t), kept)
        lseb[rows] = kept
        red1.start(c, dot_nn(ob[rows], wout[...]))

    def middle(i, c):
        sl = pl.ds(c * piece, piece)
        h1 = xbuf[i, sl].astype(F32) + red1.result(c) + vrow(2)
        h1b[sl] = h1
        hat, _ = norm_stats(h1)
        gat2.mine(c)[...] = (hat * vrow(3) + vrow(4)).astype(BF)
        gat2.start(c)

    def feed(c):
        rows = pl.ds(c * CHUNK, CHUNK)
        gat2.finish(c)
        u = dot_nt(a2b[rows], w1[...]) + vec[5:6, 0 : w1.shape[0]]
        uu = u * u
        t = jnp.tanh(GELU_SCALE * (u + GELU_CUBIC * uu * u))
        half = 0.5 * (1.0 + t)
        gb[rows] = (u * half).astype(BF)
        slb[rows] = (
            half + 0.5 * u * (1.0 - t * t) * (GELU_SCALE * (1.0 + 3.0 * GELU_CUBIC * uu))
        ).astype(BF)
        red2.start(c, dot_nn(gb[rows], w2[...]))

    def end(i, c):
        sl = pl.ds(c * piece, piece)
        outb[sl] = (h1b[sl] + red2.result(c) + vrow(6)).astype(BF)

        @pl.when(stage == 0)
        def _():
            pipe_copy(i, c).start()

        @pl.when(stage == 1)
        def _():
            y_copy(i, c).start()

    def end_wait(i, c):
        @pl.when(stage == 0)
        def _():
            pipe_copy(i, c).wait_send()

        @pl.when(stage == 1)
        def _():
            y_copy(i, c).wait()

    def saves(i):
        return [
            pltpu.make_async_copy(a, b, lsem.at[1 + n])
            for n, (a, b) in enumerate(
                (
                    (a1b.at[lax.rem(i, 2)], a1_o.at[i]),
                    (qkvb, qkv_o.at[i]),
                    (ob, o_o.at[i]),
                    (lseb, lse_o.at[i]),
                    (a2b, a2_o.at[i]),
                    (gb, g_o.at[i]),
                    (slb, sl_o.at[i]),
                    (h1b, h1_o.at[i]),
                    (xbuf.at[i], xin_o.at[i]),
                )
            )
        ]

    @pl.when(stage == 0)
    def _():
        load.wait()

    every = range(chunks)

    def first(i):
        for c in every:
            begin(i, c)

    def second(i):
        for c in every:
            gat1(i).forward(c)
        for c in every:
            project(i, c)
        for c in every:
            gat1(i).drain(c)

    first(0)
    second(0)

    def image(i, carry):
        sv = saves(i)
        sv[0].start()
        sv[1].start()
        for s in range(chunks + 6):
            def at(j):
                return s - j if 0 <= s - j < chunks else None

            c = at(0)
            if c is not None:
                attend(c)
            c = at(1)
            if c is not None:
                red1.cross(c)
            c = at(5)
            if c is not None:
                red2.cross(c)
            c = at(2)
            if c is not None:
                middle(i, c)
            c = at(3)
            if c is not None:
                gat2.forward(c)
            c = at(6)
            if c is not None:
                end(i, c)
            c = at(4)
            if c is not None:
                feed(c)
            if s == chunks:
                sv[2].start()
                sv[3].start()
        for n in range(4, 9):
            sv[n].start()
        for n in range(9):
            sv[n].wait()

        @pl.when(i + 1 < images)
        def _():
            first(i + 1)

        for c in every:
            red1.drain(c)
            red2.drain(c)
            gat2.drain(c)
            end_wait(i, c)

        @pl.when(i + 1 < images)
        def _():
            second(i + 1)

        return carry

    lax.fori_loop(0, images, image, 0)


def backward_kernel(
    images, chunks, heads, length, scaling, rows_mp, dp_n, pairs,
    d_hbm, y_in, vec, wqkv, wout, w1, w2,
    xin_i, a1_i, qkv_i, o_i, lse_i, a2_i, g_i, sl_i, h1_i,
    full_o, w2_o, w1_o, out_o, qkv_o, sums_o,
    acc, small, gbqkv, obuf, fbuf, stage_buf, land_buf, sum_buf, wide_buf, mslot, dslot, sbuf, dbuf, xinb, a1b, qkvb, ob, lseb, a2b, gb, slb, h1b, dmb, dab, dqb, dkv, dob, outb,
    part1, near1, out1, far1, part2, near2, out2, far2,
    ssem, rsem, psend, precv, lsem, agsend, agrecv, msem, mrecv, dsem, drecv, zsend, zpart, zfinal, zpass, zkeep, pcredit, fcredit,
):
    spot = Spot(rows_mp)
    stage, piece = spot.stage, spot.piece
    hw = heads * HPAD
    hid = w1.shape[0]
    z = lax.axis_index("dp")
    me = lax.axis_index("mp")
    load = pltpu.make_async_copy(d_hbm, dbuf, lsem.at[0])
    load_y = pltpu.make_async_copy(y_in, obuf, lsem.at[10])

    @pl.when(stage == 1)
    def _():
        load.start()
        load_y.start()

    def loads(i):
        return [
            pltpu.make_async_copy(b, a, lsem.at[1 + n])
            for n, (a, b) in enumerate(
                (
                    (a1b, a1_i.at[i]),
                    (qkvb, qkv_i.at[i]),
                    (ob, o_i.at[i]),
                    (lseb, lse_i.at[i]),
                    (a2b, a2_i.at[i]),
                    (gb, g_i.at[i]),
                    (slb, sl_i.at[i]),
                    (h1b, h1_i.at[i]),
                    (xinb, xin_i.at[i]),
                )
            )
        ]

    back_loads, front_loads = (7, 1, 2, 3, 0, 8), (4, 5, 6)
    for n in back_loads:
        loads(0)[n].start()
    enter(spot, dp_n)
    kinds = sem_kinds(rows_mp)
    gatm = Gather(dmb, ssem, rsem, kinds[0], spot)
    gata = Gather(dab, ssem, rsem, kinds[1], spot)
    red1 = Reduce(part1, near1, out1, far1, ssem, rsem, kinds[2], spot)
    red2 = Reduce(part2, near2, out2, far2, ssem, rsem, kinds[3], spot)
    every = range(chunks)

    acc[...] = jnp.zeros_like(acc)
    small[...] = jnp.zeros_like(small)
    gbqkv[...] = jnp.zeros_like(gbqkv)

    def add(r, v):
        small[r : r + 1, :] += v

    def pipe_copy(i, c):
        return remote(
            outb.at[pl.ds(c * piece, piece)],
            dbuf.at[i, pl.ds(c * piece, piece)],
            psend.at[c],
            precv.at[i, c],
            {"pipe": 0},
        )

    def begin(i, c):
        @pl.when(stage == 0)
        def _():
            pipe_copy(i, c).wait_recv()

        v = dbuf[i, pl.ds(c * piece, piece)]
        gatm.mine(c)[...] = v
        gatm.start(c)
        add(6, col_sum(v.astype(F32)))

    def feed(c):
        rows = pl.ds(c * CHUNK, CHUNK)
        gatm.finish(c)
        du = (dot_nt(dmb[rows], w2[...]) * slb[rows].astype(F32)).astype(BF)
        slb[rows] = du
        small[5:6, 0 : w1.shape[0]] += col_sum(du.astype(F32))
        red1.start(c, dot_nn(du, w1[...]))

    def middle(i, c):
        sl = pl.ds(c * piece, piece)
        e = red1.result(c)
        hat, inv = norm_stats(h1b[sl])
        add(3, col_sum(e * hat))
        add(4, col_sum(e))
        dh = dbuf[i, sl].astype(F32) + norm_back(e, hat, inv, vec[3:4, :])
        h1b[sl] = dh
        add(2, col_sum(dh))
        gata.mine(c)[...] = dh.astype(BF)
        gata.start(c)

    def weights(base, a, b, step):
        def tile(n, carry):
            cols = pl.ds(pl.multiple_of(n * step, step), step)
            acc[pl.ds(pl.multiple_of(base + n * step, step), step)] += dot_tn(a[:, cols], b[...])
            return carry

        lax.fori_loop(0, a.shape[1] // step, tile, 0)

    def head_weights(base, a, b):
        def group(n, carry):
            cols = pl.ds(pl.multiple_of(n * hw, HPAD), hw)
            part = dot_tn(a[:, cols], b[...])
            for h in range(heads):
                start = base + (n * heads + h) * HDIM
                acc[pl.ds(pl.multiple_of(start, 8), HDIM)] += part[h * HPAD : h * HPAD + HDIM]
            return carry

        lax.fori_loop(0, a.shape[1] // hw, group, 0)

    def attend(c, between=()):
        rows = pl.ds(c * CHUNK, CHUNK)
        total = chunks * CHUNK
        valid = lax.broadcasted_iota(jnp.int32, (CHUNK, total), 1) < length
        gata.finish(c)
        dob[...] = dot_nt(dab[rows], wout[...]).astype(BF)
        for h in range(heads):
            cq = slice(h * HPAD, (h + 1) * HPAD)
            ck = slice(hw + h * HPAD, hw + (h + 1) * HPAD)
            cv = slice(2 * hw + h * HPAD, 2 * hw + (h + 1) * HPAD)
            q, k, v = qkvb[rows, cq], qkvb[:, ck], qkvb[:, cv]
            d = dob[:, cq]
            s = dot_nt(q, k) * scaling
            p = jnp.where(valid, jnp.exp(s - lseb[rows, h : h + 1]), 0.0)
            dv = dot_tn(p.astype(BF), d)
            dp = dot_nt(d, v)
            inner = jnp.sum(dp * p, axis=-1, keepdims=True)
            ds = (p * (dp - inner)).astype(BF)
            dq = (dot_nn(ds, k) * scaling).astype(BF)
            dqb[rows, cq] = dq
            gbqkv[0:1, cq] += col_sum(dq.astype(F32))
            dk = dot_tn(ds, q)
            if c == 0:
                dkv[:, cq] = dk
                dkv[:, ck] = dv
            else:
                dkv[:, cq] += dk
                dkv[:, ck] += dv
            if h == heads // 2 - 1:
                for action in between:
                    action()

    def close():
        dk = (dkv[:, 0:hw] * scaling).astype(BF)
        dqb[:, hw : 2 * hw] = dk
        dv = dkv[:, hw : 2 * hw].astype(BF)
        dqb[:, 2 * hw : 3 * hw] = dv
        gbqkv[0:1, 2 * hw : 3 * hw] += col_sum(dv.astype(F32))

    def unproject(c):
        rows = pl.ds(c * CHUNK, CHUNK)
        red2.start(c, dot_nn(dqb[rows], wqkv[...]))

    def end(i, c):
        sl = pl.ds(c * piece, piece)
        e = red2.result(c)
        hat, inv = norm_stats(xinb[sl].astype(F32))
        add(0, col_sum(e * hat))
        add(1, col_sum(e))
        dx = (h1b[sl] + norm_back(e, hat, inv, vec[0:1, :])).astype(BF)

        @pl.when(stage == 1)
        def _():
            outb[sl] = dx
            pipe_copy(i, c).start()

        @pl.when(stage == 0)
        def _():
            obuf[i, c] = dx

    def end_wait(i, c):
        @pl.when(stage == 1)
        def _():
            pipe_copy(i, c).wait_send()

    @pl.when(stage == 1)
    def _():
        load.wait()
        load_y.wait()

    tall = stage_buf.shape[1]
    wide_units = 2 * pairs
    units = wide_units + 4 * heads
    right, left = lax.rem(z + 1, dp_n), lax.rem(z + dp_n - 1, dp_n)

    def owner(u):
        return dp_n // 2 - 1 + lax.rem(u, 2)

    def send_copy(dst, u, side, recv):
        slot = lax.rem(u, SLOTS)
        return remote(stage_buf.at[slot], dst, zsend.at[slot, side], recv, {"dp": left if side else right})

    def part_copy(u, side):
        slot = lax.rem(u, PART_SLOTS)
        return send_copy(land_buf.at[side, slot], u, side, zpart.at[side, slot])

    def sum_copy(u, side):
        slot = lax.rem(u, SUM_SLOTS)
        return send_copy(sum_buf.at[slot], u, side, zfinal.at[slot])

    def put(u, act):
        slot = lax.rem(u, 2)
        buf, sem = wide_buf.at[slot], zkeep.at[slot]

        def rows(first):
            return pl.ds(pl.multiple_of((u - first) * tall, 8), tall)

        for ref, lo, hi in ((w2_o, 0, pairs), (w1_o, pairs, wide_units)):

            @pl.when((u >= lo) & (u < hi))
            def _(ref=ref, lo=lo):
                act(pltpu.make_async_copy(buf, ref.at[rows(lo), 0], sem))

        for ref, lo, hi in ((out_o, wide_units, wide_units + heads), (qkv_o, wide_units + heads, units)):

            @pl.when((u >= lo) & (u < hi))
            def _(ref=ref, lo=lo):
                act(pltpu.make_async_copy(buf, ref.at[rows(lo)], sem))

    def emit(u, value, settled):
        @pl.when(settled)
        def _():
            put(u - 2, lambda copy: copy.wait())

        wide_buf[lax.rem(u, 2)] = value.astype(F32)
        put(u, lambda copy: copy.start())

    def pass_copy(u, side):
        slot = lax.rem(u, SUM_SLOTS)
        view = sum_buf.at[slot]
        return remote(view, view, zpass.at[slot], zfinal.at[slot], {"dp": left if side else right})

    def grant(sem, target):
        pl.semaphore_signal(sem, inc=1, device_id={"dp": target}, device_id_type=MESH)

    def sends(u, act):
        mid = owner(u)

        @pl.when((z <= mid) & (z < dp_n - 1))
        def _():
            act(0)

        @pl.when((z >= mid) & (z > 0))
        def _():
            act(1)

    def settle(u):
        sends(u, lambda side: part_copy(u, side).wait_send())

    def start_sum(copy, u, side):
        @pl.when(u >= SUM_SLOTS)
        def _():
            pl.semaphore_wait(fcredit.at[side, lax.rem(u, 2)], 1)

        copy.start()

    def start_part(u, side):
        @pl.when(u >= PART_SLOTS)
        def _():
            pl.semaphore_wait(pcredit.at[side, lax.rem(u, 2)], 1)

        part_copy(u, side).start()

    def reduce_unit(u, value):
        mid = owner(u)
        from_left = (z > 0) & (z <= mid)
        from_right = (z < dp_n - 1) & (z >= mid)
        for side, cond in ((0, from_left), (1, from_right)):

            @pl.when(cond)
            def _(side=side):
                part_copy(u, side).wait_recv()

            value = value + jnp.where(cond, land_buf[side, lax.rem(u, PART_SLOTS)].astype(F32), 0.0)

        @pl.when(u >= SLOTS)
        def _():
            settle(u - SLOTS)

        stage_buf[lax.rem(u, SLOTS)] = value.astype(BF)
        for side, cond in ((0, from_left), (1, from_right)):

            @pl.when(cond & (u + PART_SLOTS < units))
            def _(side=side):
                grant(pcredit.at[side, lax.rem(u, 2)], right if side else left)

        @pl.when(z == mid)
        def _():
            sends(u, lambda side: start_sum(sum_copy(u, side), u, side))
            emit(u, stage_buf[lax.rem(u, SLOTS)], u >= 2)

        @pl.when(z != mid)
        def _():
            sends(u, lambda side: start_part(u, side))

    def release(u):
        mid = owner(u)

        @pl.when(((z < mid) & (z > 0)) | ((z > mid) & (z < dp_n - 1)))
        def _():
            pass_copy(u, 0).wait_send()

        @pl.when((z < mid) & (u + SUM_SLOTS < units))
        def _():
            grant(fcredit.at[1, lax.rem(u, 2)], right)

        @pl.when((z > mid) & (u + SUM_SLOTS < units))
        def _():
            grant(fcredit.at[0, lax.rem(u, 2)], left)

    def spread_unit(u):
        mid = owner(u)

        @pl.when(z != mid)
        def _():
            sum_copy(u, 0).wait_recv()

            @pl.when((z < mid) & (z > 0))
            def _():
                start_sum(pass_copy(u, 1), u, 1)

            @pl.when((z > mid) & (z < dp_n - 1))
            def _():
                start_sum(pass_copy(u, 0), u, 0)

            emit(u, sum_buf[lax.rem(u, SUM_SLOTS)], u >= 2)

            @pl.when(u >= 2)
            def _():
                release(u - 2)

    half = dp_n // 2

    def unit(t, carry):
        mid = owner(t)
        late = t - SKEW * (half + jnp.abs(z - mid))
        now = t - SKEW * jnp.where(z < mid, z, jnp.where(z > mid, dp_n - 1 - z, half))

        @pl.when((z != mid) & (late >= 0) & (late < units))
        def _():
            spread_unit(late)

        @pl.when((now >= 0) & (now < wide_units))
        def _():
            start = now * tall + lax.div(now, pairs) * (hid - pairs * tall)
            reduce_unit(now, acc[pl.ds(pl.multiple_of(start, 8), tall)])

        @pl.when((now >= wide_units) & (now < units))
        def _():
            start = 2 * hid + (now - wide_units) * tall
            reduce_unit(now, acc[pl.ds(pl.multiple_of(start, 8), tall)])

        return carry

    def slot(s, carry):
        b, f = s - 1, s
        has_b, has_f = b >= 0, f < images
        back, front = pl.when(has_b), pl.when(has_f)
        early, late = pl.when(has_f & (stage == 1)), pl.when(has_f & (stage == 0))

        def chain(lo, hi):
            @pl.when(b == images - 1)
            def _():
                lax.fori_loop(lo, hi, unit, 0)

        @back
        def _():
            loads(b)[7].wait()
            for c in every:
                middle(b, c)
            for c in every:
                red1.drain(c)
            weights(hid, slb, a2b, tile_of(hid))

        chain(0, 2)

        @front
        def _():
            for n in front_loads:
                loads(f)[n].start()

        @back
        def _():
            for n in (0, 1, 2, 3, 8):
                loads(b)[n].wait()
            gata.forward(0)
            attend(0, [functools.partial(gata.forward, c) for c in range(1, chunks - 1)])

        @early
        def _():
            for c in every:
                begin(f, c)

        def pass_early():
            @early
            def _():
                for c in range(chunks - 1):
                    gatm.forward(c)

        chain(2, 5)

        @back
        def _():
            gata.forward(chunks - 1)
            for c in range(1, chunks - 1):
                attend(c)

        chain(5, 8)

        @back
        def _():
            attend(chunks - 1, [pass_early])

        @pl.when(has_f & jnp.logical_not(has_b))
        def _():
            pass_early()

        chain(8, 11)

        @back
        def _():
            close()
            for c in range(chunks - 1):
                unproject(c)
                if c >= 1:
                    red2.cross(c - 1)
            head_weights(2 * hid, ob, dab)
            for c in every:
                gata.drain(c)
            unproject(chunks - 1)
            red2.cross(chunks - 2)

        @late
        def _():
            for c in every:
                begin(f, c)
            for c in range(chunks - 1):
                gatm.forward(c)

        @front
        def _():
            gatm.forward(chunks - 1)
            for n in front_loads:
                loads(f)[n].wait()

        chain(11, 14)
        for c in every:

            @front
            def _():
                feed(c)

            @back
            def _():
                if c == 0:
                    red2.cross(chunks - 1)
                end(b, c)

            @front
            def _():
                red1.cross(c)

        @pl.when(has_b & (b + 1 < images))
        def _():
            loads(b + 1)[back_loads[0]].start()

        @front
        def _():
            for c in every:
                gatm.drain(c)
            weights(0, gb, dmb, tile_of(hid))

        chain(14, AHEAD)

        @back
        def _():
            head_weights(2 * hid + heads * HDIM, dqb, a1b)
            for c in every:
                red2.drain(c)
                end_wait(b, c)

        @pl.when(has_b & (b + 1 < images))
        def _():
            for n in back_loads[1:]:
                loads(b + 1)[n].start()

        return carry

    lax.fori_loop(0, images + 1, slot, 0)

    def block(core, row):
        return full_o.at[:, :, core * rows_mp + row]

    ag_own = pltpu.make_async_copy(obuf, block(spot.core, spot.row), lsem.at[0])

    def ag_near():
        return remote(obuf, block(spot.core, spot.row), agsend.at[0], agrecv.at[0], {"mp": spot.sib})

    def ag_far(j):
        k = 2 * j - 1
        return remote(obuf, fbuf.at[j - 1], agsend.at[k], agrecv.at[k], spot.peer(spot.ahead(j)))

    def ag_pass(j):
        view = block(spot.core, spot.behind(j))
        return remote(fbuf.at[j - 1], view, agsend.at[2 * j], agrecv.at[2 * j], {"mp": spot.sib})

    def ag_keep(j):
        return pltpu.make_async_copy(fbuf.at[j - 1], block(spot.core, spot.behind(j)), lsem.at[3 + j])

    ag_own.start()
    for j in range(1, rows_mp):
        ag_far(j).start()
    ag_near().start()

    mp_n = 2 * rows_mp

    def mp_copy(j):
        return remote(small, mslot.at[me], msem.at[j - 1], mrecv.at[j - 1], {"mp": lax.rem(me + j, mp_n)})

    def dp_copy(j):
        return remote(sbuf, dslot.at[z], dsem.at[j - 1], drecv.at[j - 1], {"dp": lax.rem(z + j, dp_n)})

    for j in range(1, mp_n):
        mp_copy(j).start()
    mslot[me] = small[...]
    for j in range(1, mp_n):
        mp_copy(j).wait_recv()
    total = mslot[0]
    for j in range(1, mp_n):
        total = total + mslot[j]
    own_row = lax.broadcasted_iota(jnp.int32, total.shape, 0) == 5
    sbuf[0:8] = jnp.where(own_row, small[...], total)
    sbuf[8:16] = jnp.zeros_like(total)
    sbuf[8:9, 0:hw] = gbqkv[0:1, 0:hw]
    sbuf[9:10, 0:hw] = gbqkv[0:1, 2 * hw : 3 * hw]
    for j in range(1, dp_n):
        dp_copy(j).start()
    dslot[z] = sbuf[...]

    for j in range(1, dp_n):
        dp_copy(j).wait_recv()
    total = dslot[0]
    for j in range(1, dp_n):
        total = total + dslot[j]
    sums_o[...] = total
    lax.fori_loop(AHEAD, AHEAD + 4, unit, 0)
    for j in range(1, rows_mp):
        ag_far(j).wait_recv()
        ag_pass(j).start()
        ag_keep(j).start()
    lax.fori_loop(AHEAD + 4, units + SKEW * dp_n, unit, 0)

    def last(t, carry):
        settle(t)
        return carry

    lax.fori_loop(units - SLOTS, units, last, 0)

    def freed(u, carry):
        put(u, lambda copy: copy.wait())

        @pl.when(z != owner(u))
        def _():
            release(u)

        return carry

    lax.fori_loop(units - 2, units, freed, 0)
    ag_own.wait()
    ag_near().wait_send()
    ag_near().wait_recv()
    for j in range(1, rows_mp):
        ag_far(j).wait_send()
        ag_pass(j).wait_send()
        ag_pass(j).wait_recv()
        ag_keep(j).wait()
    for j in range(1, mp_n):
        mp_copy(j).wait_send()
    for j in range(1, dp_n):
        dp_copy(j).wait_send()


def vmem():
    return pl.BlockSpec(memory_space=pltpu.VMEM)


def anywhere():
    return pl.BlockSpec(memory_space=pl.ANY)


def comm_scratch(chunks, width, rows_mp):
    one = [
        pltpu.VMEM((chunks, CHUNK, width), BF),
        pltpu.VMEM((chunks, HALF, width), BF),
        pltpu.VMEM((chunks, rows_mp - 1, HALF // rows_mp, width), BF),
        pltpu.VMEM((chunks, rows_mp - 1, HALF // rows_mp, width), BF),
    ]
    return one + one


def sem_kinds(rows_mp):
    gather = 2 * rows_mp - 1
    return 0, gather, 2 * gather, 2 * gather + rows_mp


def sems(images, chunks, rows_mp):
    dma = pltpu.SemaphoreType.DMA
    kinds = 6 * rows_mp - 2
    return [dma((kinds, chunks)), dma((kinds, chunks)), dma((chunks,)), dma((images, chunks)), dma((11,))]


def on_device(
    section_in,
    ln1_gain,
    ln1_bias,
    qkv_weight,
    qv_bias,
    out_weight,
    out_bias,
    ln2_gain,
    ln2_bias,
    fc1_weight,
    fc1_bias,
    fc2_weight,
    fc2_bias,
):
    stage = lax.axis_index("pipe")
    me = lax.axis_index("mp")
    rows_in = section_in[0]
    images, length, width = rows_in.shape
    cols = out_weight.shape[1]
    heads = cols // HDIM
    hidden = fc1_weight.shape[2]
    hid = -(-hidden // HPAD) * HPAD
    chunks = -(-length // CHUNK)
    total = chunks * CHUNK
    hw = heads * HPAD
    scaling = HDIM ** (-0.5)
    rows_mp = lax.axis_size("mp") // 2
    piece = HALF // rows_mp
    pos = lax.rem(me, 2) * rows_mp + lax.div(me, 2)

    padded = jnp.pad(rows_in, ((0, 0), (0, total - length), (0, 0)))
    mine = lax.dynamic_index_in_dim(
        padded.reshape(images, chunks, 2 * rows_mp, piece, width), pos, 2, keepdims=False
    ).reshape(images, chunks * piece, width)

    def row_of(v):
        v = v.reshape(1, -1).astype(F32)
        return jnp.pad(v, ((0, 0), (0, width - v.shape[1])))

    vec = jnp.concatenate(
        [
            row_of(ln1_gain),
            row_of(ln1_bias),
            row_of(out_bias),
            row_of(ln2_gain),
            row_of(ln2_bias),
            row_of(fc1_bias),
            row_of(fc2_bias),
            jnp.zeros((1, width), F32),
        ]
    )
    lanes = ((0, 0), (0, 0), (0, 0), (0, HPAD - HDIM))
    tall = ((0, 0), (0, HPAD - HDIM), (0, 0))
    wqkv = jnp.transpose(qkv_weight[0], (1, 2, 0)).reshape(3 * heads, HDIM, width)
    wqkv = jnp.pad(wqkv, tall).reshape(3 * hw, width)
    bias_three = jnp.stack([qv_bias[0, 0], jnp.zeros_like(qv_bias[0, 0]), qv_bias[0, 1]])
    bqkv = jnp.pad(bias_three.reshape(1, 3, heads, HDIM), lanes).reshape(1, 3 * hw).astype(F32)
    wout = jnp.pad(out_weight[0].reshape(heads, HDIM, width), tall).reshape(hw, width)
    w1 = jnp.pad(fc1_weight[0].T, ((0, hid - hidden), (0, 0)))
    w2 = jnp.pad(fc2_weight[0], ((0, hid - hidden), (0, 0)))

    def arr(*shape, dtype=BF):
        return jax.ShapeDtypeStruct(shape, dtype)

    own = chunks * piece
    kept_shapes = [
        arr(images, own, width),
        arr(images, total, width),
        arr(images, total, 3 * hw),
        arr(images, total, hw),
        arr(images, total, HPAD, dtype=F32),
        arr(images, total, width),
        arr(images, total, hid),
        arr(images, total, hid),
        arr(images, own, width, dtype=F32),
    ]
    kept_vmem = [
        pltpu.VMEM((total, 3 * hw), BF),
        pltpu.VMEM((total, hw), BF),
        pltpu.VMEM((total, HPAD), F32),
        pltpu.VMEM((total, width), BF),
        pltpu.VMEM((total, hid), BF),
        pltpu.VMEM((total, hid), BF),
        pltpu.VMEM((own, width), F32),
    ]
    y_mine, *kept = pl.pallas_call(
        functools.partial(forward_kernel, images, chunks, heads, length, scaling, rows_mp),
        out_shape=[arr(images, own, width)] + kept_shapes,
        in_specs=[anywhere()] + [vmem()] * 6,
        out_specs=[anywhere()] * 10,
        scratch_shapes=[
            pltpu.VMEM((images, own, width), BF),
            pltpu.VMEM((2, total, width), BF),
            *kept_vmem,
            pltpu.VMEM((own, width), BF),
            *comm_scratch(chunks, width, rows_mp),
            *sems(images, chunks, rows_mp),
        ],
        compiler_params=pltpu.CompilerParams(
            collective_id=0, has_side_effects=True, vmem_limit_bytes=VMEM_LIMIT
        ),
        name="layer_forward",
    )(mine, vec, bqkv, wqkv, wout, w1, w2)

    dp_n = lax.axis_size("dp")
    tall_unit = HDIM
    pairs = -(-hidden // tall_unit)
    dma = pltpu.SemaphoreType.DMA
    full, g2, g1, gout, gqkv, sums = pl.pallas_call(
        functools.partial(backward_kernel, images, chunks, heads, length, scaling, rows_mp, dp_n, pairs),
        out_shape=[
            arr(images, chunks, 2 * rows_mp, piece, width),
            arr(pairs * tall_unit, 1, width, dtype=F32),
            arr(pairs * tall_unit, 1, width, dtype=F32),
            arr(cols, width, dtype=F32),
            arr(3 * cols, width, dtype=F32),
            arr(16, width, dtype=F32),
        ],
        in_specs=[anywhere()] * 2 + [vmem()] * 5 + [anywhere()] * 9,
        out_specs=[anywhere()] * 5 + [vmem()],
        scratch_shapes=[
            pltpu.VMEM((2 * hid + 4 * cols, width), F32),
            pltpu.VMEM((8, width), F32),
            pltpu.VMEM((1, 3 * hw), F32),
            pltpu.VMEM((images, chunks, piece, width), BF),
            pltpu.VMEM((rows_mp - 1, images, chunks, piece, width), BF),
            pltpu.VMEM((SLOTS, tall_unit, width), BF),
            pltpu.VMEM((2, PART_SLOTS, tall_unit, width), BF),
            pltpu.VMEM((SUM_SLOTS, tall_unit, width), BF),
            pltpu.VMEM((2, tall_unit, width), F32),
            pltpu.VMEM((2 * rows_mp, 8, width), F32),
            pltpu.VMEM((dp_n, 16, width), F32),
            pltpu.VMEM((16, width), F32),
            pltpu.VMEM((images, own, width), BF),
            pltpu.VMEM((own, width), BF),
            pltpu.VMEM((total, width), BF),
            *kept_vmem,
            pltpu.VMEM((total, width), BF),
            pltpu.VMEM((total, width), BF),
            pltpu.VMEM((total, 3 * hw), BF),
            pltpu.VMEM((total, 2 * hw), F32),
            pltpu.VMEM((CHUNK, hw), BF),
            pltpu.VMEM((own, width), BF),
            *comm_scratch(chunks, width, rows_mp),
            *sems(images, chunks, rows_mp),
            dma((2 * rows_mp - 1,)),
            dma((2 * rows_mp - 1,)),
            dma((2 * rows_mp - 1,)),
            dma((2 * rows_mp - 1,)),
            dma((dp_n - 1,)),
            dma((dp_n - 1,)),
            dma((SLOTS, 3)),
            dma((2, PART_SLOTS)),
            dma((SUM_SLOTS,)),
            dma((SUM_SLOTS,)),
            dma((SUM_SLOTS,)),
            pltpu.SemaphoreType.REGULAR((2, 2)),
            pltpu.SemaphoreType.REGULAR((2, 2)),
        ],
        compiler_params=pltpu.CompilerParams(
            collective_id=1, has_side_effects=True, vmem_limit_bytes=VMEM_LIMIT
        ),
        name="layer_backward",
    )(mine, y_mine.reshape(images, chunks, piece, width), vec, wqkv, wout, w1, w2, *kept)

    section_out = full.reshape(images, total, width)[:, :length][None]
    g2, g1 = jnp.transpose(g2[:hidden], (1, 0, 2)), jnp.transpose(g1[:hidden], (1, 2, 0))
    gqkv = jnp.transpose(gqkv.reshape(3, cols, width), (2, 0, 1))
    gb = sums[8:10, :hw].reshape(2, heads, HPAD)[:, :, :HDIM].reshape(1, 2, cols)
    return (
        section_out,
        sums[0:1],
        sums[1:2],
        gqkv[None],
        gb,
        gout[None],
        sums[2:3],
        sums[3:4],
        sums[4:5],
        g1,
        sums[5:6, :hidden],
        g2,
        sums[6:7],
    )


def solution(mesh):
    vector, matrix = P("pipe", None), P("pipe", "mp", None)
    acts = P("pipe", "dp", None, None)
    heads = P("pipe", None, None, "mp")
    pair = P("pipe", None, "mp")
    params = (vector, vector, heads, pair, matrix, vector, vector, vector, pair, P("pipe", "mp"), matrix, vector)
    return jax.shard_map(
        on_device,
        mesh=mesh,
        in_specs=(acts, *params),
        out_specs=(acts, *params),
        check_vma=False,
    )
```
